256 devices in a mesh: dp: 8 (over y, core), ctx: 32 (over x, z).
Axes of the slice: x: 4, y: 4, z: 8, core: 2. Of those that a mesh axis runs over, the one named last changes fastest.
Arguments:
- queries: bfloat16 [8, 8192, 2560], P('dp', 'ctx'), may hold values from -120 to 120
- global_keys: bfloat16 [8, 8192, 512], P('dp', 'ctx'), may hold values from -5 to 5
- global_values: bfloat16 [8, 8192, 512], P('dp', 'ctx'), may hold values from -6 to 6
- out_grad: bfloat16 [8, 8192, 2560], P('dp', 'ctx'), may hold values from -6 to 6
- query_gain: float32 [2560], replicated, may hold values from 0.5 to 1.5
- doc_start: int32 [8, 64], P('dp', 'ctx'), may hold values from 0 to 63, as said below
Outputs:
- attn_out: bfloat16 [8, 8192, 2560], P('dp', 'ctx')
- query_grad: bfloat16 [8, 8192, 2560], P('dp', 'ctx')
- key_grad: bfloat16 [8, 8192, 512], P('dp', 'ctx')
- value_grad: bfloat16 [8, 8192, 512], P('dp', 'ctx')
- gain_grad: float32 [2560], replicated
The draws below stay inside these ranges and needn't reach their ends.
Inputs may be any that keep to these rules, and one draw needn't show every extreme that they name: doc_start[g, b] is the first block of block b's document: it is at most b and at least b - 6, never falls along b, and equals b where a document begins; every slab has a document of exactly 7 blocks.
All inputs are finite; a program needn't handle non-finite values.
Results may differ from the reference program's by a relative error of at most 0.017.
The reference program's roundings to bfloat16 on the way count: a program that leaves them out, or rounds other values in their place, can miss the bound.
Values may be sent and summed in bfloat16 or wider, within the bound.
No kernel may reach another device: no remote copies, remote signals or barrier semaphores. Data moves between devices by JAX's collectives and lax.ppermute only.
A program may use at most 64 MiB of HBM per device.

```python
import math
import jax
import jax.numpy as jnp
from jax import lax

HEADS = 20
KV_HEADS = 4
HD = 128
BLOCK = 128
REACH = 4
TOK_DEV = 256
GROUPS = 8
SEQ = 8192
DOC_BLOCKS = 7
N_CTX = 32


def shared_keys(key):
    raw = jax.random.normal(jax.random.fold_in(key, 7), (GROUPS, SEQ, KV_HEADS * HD), jnp.float32)
    return jnp.clip(raw, -5.0, 5.0)


def draw_global_keys(key, part):
    base = shared_keys(key)
    return base.astype(jnp.bfloat16)


def draw_queries(key, part):
    drawn = jax.random.normal(jax.random.fold_in(key, 13), (GROUPS, SEQ, HEADS * HD), jnp.float32)
    drawn = jnp.clip(drawn, -5.0, 5.0)
    return drawn.astype(jnp.bfloat16)


def draw_doc_start(key, part):
    count = SEQ // BLOCK

    def one_group(group_key):
        lengths = jax.random.randint(jax.random.fold_in(group_key, 1), (count,), 1, DOC_BLOCKS + 1)
        longest = jax.random.randint(jax.random.fold_in(group_key, 2), (), 0, count // DOC_BLOCKS)
        lengths = jnp.where(jnp.arange(count) == longest, DOC_BLOCKS, lengths)
        starts = jnp.cumsum(lengths) - lengths
        blocks = jnp.arange(count)
        return jnp.max(jnp.where(starts[None, :] <= blocks[:, None], starts[None, :], 0), axis=1)
    group_keys = jax.vmap(lambda index: jax.random.fold_in(key, index))(jnp.arange(GROUPS))
    return jax.vmap(one_group)(group_keys).astype(jnp.int32)


def levels(own_key, dims, split, smallest, top_value):
    factor_of = 1.0
    for position, shards_of in split:
        heights = jax.random.uniform(jax.random.fold_in(jax.random.fold_in(own_key, 6), position), (shards_of,), jnp.float32, smallest / len(split), top_value / len(split))
        factor_of = factor_of * jnp.repeat(jnp.exp(heights), dims[position] // shards_of).reshape((-1,) + (1,) * (len(dims) - 1 - position))
    return factor_of


def centred(key, shape, scale, bound, shards=(), held_as=jnp.bfloat16):
    values = scale * jax.random.normal(key, shape, jnp.float32)
    if shards:
        values = values * levels(key, shape, shards, -0.22, 0.18)
    return jnp.clip(values, -bound, bound).astype(held_as)


def setup_inputs(seed: int = 0) -> dict:
    key_of = jax.random.split(jax.random.key(seed), 7)
    queries = draw_queries(jax.random.fold_in(key_of[6], 71), 0)
    global_keys = draw_global_keys(jax.random.fold_in(key_of[6], 71), 0)
    global_values = centred(key_of[2], (GROUPS, SEQ, KV_HEADS * HD), 1.0, 6.0, ((0, 8), (1, 32)))
    out_grad = centred(key_of[3], (GROUPS, SEQ, HEADS * HD), 1.0, 6.0, ((0, 8), (1, 32)))
    query_gain = jnp.clip(1.0 + 0.1 * jax.random.normal(key_of[4], (HEADS * HD,), jnp.float32), 0.5, 1.5)
    doc_start = draw_doc_start(jax.random.fold_in(key_of[6], 71), 0)
    return {"queries": queries, "global_keys": global_keys, "global_values": global_values, "out_grad": out_grad, "query_gain": query_gain, "doc_start": doc_start}


def core_block(query_block, key_window, value_window, grad_block, allowed):
    kv_count = key_window.shape[1] // HD
    group_size = query_block.shape[1] // (kv_count * HD)
    factor = 1.0 / math.sqrt(HD)
    query_four = query_block.astype(jnp.float32).reshape(query_block.shape[0], kv_count, group_size, HD)
    grad_four = grad_block.astype(jnp.float32).reshape(grad_block.shape[0], kv_count, group_size, HD)
    key_three = key_window.astype(jnp.float32).reshape(key_window.shape[0], kv_count, HD)
    value_three = value_window.astype(jnp.float32).reshape(value_window.shape[0], kv_count, HD)
    scores = jnp.einsum('tcgd,wcd->cgtw', query_four, key_three) * factor
    scores = jnp.where(allowed[None, None], scores, -jnp.inf)
    row_max = lax.optimization_barrier(jnp.max(scores, axis=-1, keepdims=True))
    log_total = row_max + jnp.log(lax.optimization_barrier(jnp.sum(jnp.exp(scores - row_max), axis=-1, keepdims=True)))
    weights = jnp.exp(scores - log_total)
    weights_low = weights.astype(jnp.bfloat16).astype(jnp.float32)
    result = jnp.einsum('cgtw,wcd->tcgd', weights_low, value_three).astype(jnp.bfloat16)
    inner_sum = lax.optimization_barrier(jnp.sum(grad_four * result.astype(jnp.float32), axis=-1))
    inner_sum = jnp.transpose(inner_sum, (1, 2, 0))
    dweights = jnp.einsum('tcgd,wcd->cgtw', grad_four, value_three)
    dscore = weights * (dweights - inner_sum[..., None])
    dscore_low = dscore.astype(jnp.bfloat16).astype(jnp.float32)
    dquery = jnp.einsum('cgtw,wcd->tcgd', dscore_low, key_three) * factor
    dkey = jnp.einsum('cgtw,tcgd->wcd', dscore_low, query_four) * factor
    dvalue = jnp.einsum('cgtw,tcgd->wcd', weights_low, grad_four)
    row_count = query_block.shape[0]
    width = key_window.shape[0]
    return (result.reshape(row_count, -1), dquery.reshape(row_count, -1), dkey.reshape(width, -1), dvalue.reshape(width, -1))

def one_slab(inputs, query_gain):
    queries, global_keys, global_values, out_grad, doc_start = inputs
    scaled = (queries.astype(jnp.float32) * query_gain).astype(jnp.bfloat16)
    width = REACH * TOK_DEV
    lead_rows = (REACH - 1) * TOK_DEV
    channels = global_keys.shape[1]
    padded_keys = jnp.concatenate([jnp.zeros((lead_rows, channels), jnp.bfloat16), global_keys], axis=0)
    padded_values = jnp.concatenate([jnp.zeros((lead_rows, channels), jnp.bfloat16), global_values], axis=0)
    begins = jnp.repeat(doc_start, BLOCK).astype(jnp.int32) * BLOCK

    def step(carry, device):
        key_acc, value_acc = carry
        base = (device * TOK_DEV).astype(jnp.int32)
        query_block = lax.dynamic_slice_in_dim(scaled, base, TOK_DEV, 0)
        grad_block = lax.dynamic_slice_in_dim(out_grad, base, TOK_DEV, 0)
        key_window = lax.dynamic_slice_in_dim(padded_keys, base, width, 0)
        value_window = lax.dynamic_slice_in_dim(padded_values, base, width, 0)
        query_pos = base + jnp.arange(TOK_DEV, dtype=jnp.int32)
        key_pos = base - lead_rows + jnp.arange(width, dtype=jnp.int32)
        first = lax.dynamic_slice_in_dim(begins, base, TOK_DEV, 0)
        allowed = (key_pos[None, :] <= query_pos[:, None]) & (key_pos[None, :] >= first[:, None])
        result, dquery, dkey, dvalue = core_block(query_block, key_window, value_window, grad_block, allowed)
        key_acc = lax.dynamic_update_slice_in_dim(key_acc, lax.dynamic_slice_in_dim(key_acc, base, width, 0) + dkey, base, 0)
        value_acc = lax.dynamic_update_slice_in_dim(value_acc, lax.dynamic_slice_in_dim(value_acc, base, width, 0) + dvalue, base, 0)
        return ((key_acc, value_acc), (result, dquery))
    start_acc = jnp.zeros((lead_rows + SEQ, channels), jnp.float32)
    (key_acc, value_acc), (results, dqueries) = lax.scan(step, (start_acc, start_acc), jnp.arange(N_CTX, dtype=jnp.int32))
    attn_out = results.reshape(SEQ, -1)
    dscaled = dqueries.reshape(SEQ, -1)
    query_grad = (dscaled * query_gain).astype(jnp.bfloat16)
    gain_term = lax.optimization_barrier(jnp.sum(dscaled * queries.astype(jnp.float32), axis=0))
    return (attn_out, query_grad, key_acc[lead_rows:].astype(jnp.bfloat16), value_acc[lead_rows:].astype(jnp.bfloat16), gain_term)

def reference(queries, global_keys, global_values, out_grad, query_gain, doc_start):
    attn_out, query_grad, key_grad, value_grad, gain_terms = lax.map(lambda inputs: one_slab(inputs, query_gain), (queries, global_keys, global_values, out_grad, doc_start))
    return (attn_out, query_grad, key_grad, value_grad, lax.optimization_barrier(jnp.sum(gain_terms, axis=0)))
```

```python
import functools
import math

import jax
import jax.numpy as jnp
from jax import lax
from jax.experimental import pallas as pl
from jax.experimental.pallas import tpu as pltpu
from jax.sharding import PartitionSpec as P

HD = 128
BLOCK = 128
REACH = 4
LOG2E = 1.4426950408889634


def shifted(value, axis, steps):
    count = lax.axis_size(axis)
    first, last = (max(0, -steps), min(count, count - steps))
    return lax.ppermute(value, axis, [(source, source + steps) for source in range(first, last)])


def all_sum(value, axis):
    count = lax.axis_size(axis)
    step = 1
    while step < count:
        value = value + lax.ppermute(value, axis, [(i, i ^ step) for i in range(count)])
        step *= 2
    return value


def dot(a, b, dims=((1,), (0,))):
    return lax.dot_general(a, b, (dims, ((), ())), preferred_element_type=jnp.float32)


def probs_kernel(group, rows, lo, q_ref, g_ref, gain_ref, *refs):
    k_refs, (p_ref, *dv_refs) = refs[:REACH], refs[REACH : 2 * REACH + 1]
    bias, k_all, p_low, g_all = refs[2 * REACH + 1 :]
    width = REACH * rows

    @pl.when(pl.program_id(0) == 0)
    def _():
        key = lax.broadcasted_iota(jnp.int32, (width, rows), 0)
        query = lax.broadcasted_iota(jnp.int32, (width, rows), 1)
        begin = jnp.where(query < BLOCK, lo[0], lo[1])
        allowed = (key >= begin) & (key <= query + (width - rows))
        bias[...] = jnp.where(allowed, 0.0, -jnp.inf)

    for j in range(REACH):
        k_all[j * rows : (j + 1) * rows, :] = k_refs[j][...]
    for g in range(group):
        cols = slice(g * HD, (g + 1) * HD)
        g_all[g * rows : (g + 1) * rows, :] = g_ref[:, cols]
        scaled = (q_ref[:, cols].astype(jnp.float32) * gain_ref[:, cols]).astype(jnp.bfloat16)
        raw = dot(k_all[...], scaled, ((1,), (1,))) + bias[...]
        top = jnp.max(raw, axis=0, keepdims=True)
        e = jnp.exp2((raw - top) * (LOG2E / math.sqrt(HD)))
        probs = e * (1.0 / jnp.sum(e, axis=0, keepdims=True))
        p_ref[g] = probs
        p_low[:, g * rows : (g + 1) * rows] = probs.astype(jnp.bfloat16)
    dv = dot(p_low[...], g_all[...])
    for j in range(REACH):
        dv_refs[j][...] = dv[j * rows : (j + 1) * rows, :]


def grads_kernel(group, rows, q_ref, g_ref, gain_ref, p_ref, *refs):
    k_refs, v_refs = refs[:REACH], refs[REACH : 2 * REACH]
    o_ref, dq_ref, gain_out, *dk_refs = refs[2 * REACH : 3 * REACH + 3]
    k_t, v_t, v_all, ds_all, q_all = refs[3 * REACH + 3 :]
    factor = 1.0 / math.sqrt(HD)
    for j in range(REACH):
        part = slice(j * rows, (j + 1) * rows)
        v_all[part, :] = v_refs[j][...]
        k_t[:, part] = k_refs[j][...].T
        v_t[:, part] = v_refs[j][...].T
    for g in range(group):
        cols = slice(g * HD, (g + 1) * HD)
        q32 = q_ref[:, cols].astype(jnp.float32)
        gain = gain_ref[:, cols]
        q_all[g * rows : (g + 1) * rows, :] = (q32 * gain).astype(jnp.bfloat16)
        probs = p_ref[g]
        out_t = dot(v_t[...], probs.astype(jnp.bfloat16)).astype(jnp.bfloat16)
        o_ref[:, cols] = out_t.T
        g_t = g_ref[:, cols].T
        delta = jnp.sum(g_t.astype(jnp.float32) * out_t.astype(jnp.float32), axis=0, keepdims=True)
        ds = (probs * (dot(v_all[...], g_t) - delta)).astype(jnp.bfloat16)
        ds_all[:, g * rows : (g + 1) * rows] = ds
        dscaled = (dot(k_t[...], ds) * factor).T
        dq_ref[:, cols] = (dscaled * gain).astype(jnp.bfloat16)
        gain_out[:, cols] = jnp.sum(dscaled * q32, axis=0, keepdims=True)
    dk = dot(ds_all[...], q_all[...]) * factor
    for j in range(REACH):
        dk_refs[j][...] = dk[j * rows : (j + 1) * rows, :]


def attention_probs(lo, queries, out_grad, gain, keys):
    rows, channels = queries.shape
    kv_channels = keys[0].shape[1]
    kv_count = kv_channels // HD
    group = channels // kv_channels
    width = REACH * rows
    wide = pl.BlockSpec((rows, group * HD), lambda c, lo: (0, c))
    thin = pl.BlockSpec((rows, HD), lambda c, lo: (0, c))
    return pl.pallas_call(
        functools.partial(probs_kernel, group, rows),
        out_shape=[jax.ShapeDtypeStruct((kv_count * group, width, rows), jnp.float32)]
        + [jax.ShapeDtypeStruct((rows, kv_channels), jnp.float32)] * REACH,
        grid_spec=pltpu.PrefetchScalarGridSpec(
            num_scalar_prefetch=1,
            grid=(kv_count,),
            in_specs=[wide, wide, pl.BlockSpec((1, group * HD), lambda c, lo: (0, c))]
            + [thin] * REACH,
            out_specs=[pl.BlockSpec((group, width, rows), lambda c, lo: (c, 0, 0))] + [thin] * REACH,
            scratch_shapes=[
                pltpu.VMEM((width, rows), jnp.float32),
                pltpu.VMEM((width, HD), jnp.bfloat16),
                pltpu.VMEM((width, group * rows), jnp.bfloat16),
                pltpu.VMEM((group * rows, HD), jnp.bfloat16),
            ],
        ),
        cost_estimate=pl.CostEstimate(
            flops=4 * kv_count * group * width * rows * HD,
            bytes_accessed=4 * kv_count * group * width * rows,
            transcendentals=kv_count * group * width * rows,
        ),
        name="probs",
    )(lo, queries, out_grad, gain, *keys)


def attention_grads(queries, out_grad, gain, probs, keys, values):
    rows, channels = queries.shape
    kv_channels = keys[0].shape[1]
    kv_count = kv_channels // HD
    group = channels // kv_channels
    width = REACH * rows
    wide = pl.BlockSpec((rows, group * HD), lambda c: (0, c))
    line = pl.BlockSpec((1, group * HD), lambda c: (0, c))
    thin = pl.BlockSpec((rows, HD), lambda c: (0, c))
    return pl.pallas_call(
        functools.partial(grads_kernel, group, rows),
        out_shape=[jax.ShapeDtypeStruct((rows, channels), jnp.bfloat16)] * 2
        + [jax.ShapeDtypeStruct((1, channels), jnp.float32)]
        + [jax.ShapeDtypeStruct((rows, kv_channels), jnp.float32)] * REACH,
        grid=(kv_count,),
        in_specs=[wide, wide, line, pl.BlockSpec((group, width, rows), lambda c: (c, 0, 0))]
        + [thin] * (2 * REACH),
        out_specs=[wide, wide, line] + [thin] * REACH,
        scratch_shapes=[
            pltpu.VMEM((HD, width), jnp.bfloat16),
            pltpu.VMEM((HD, width), jnp.bfloat16),
            pltpu.VMEM((width, HD), jnp.bfloat16),
            pltpu.VMEM((width, group * rows), jnp.bfloat16),
            pltpu.VMEM((group * rows, HD), jnp.bfloat16),
        ],
        cost_estimate=pl.CostEstimate(
            flops=8 * kv_count * group * width * rows * HD,
            bytes_accessed=4 * kv_count * group * width * rows,
            transcendentals=0,
        ),
        name="grads",
    )(queries, out_grad, gain, probs, *keys, *values)


def local(queries, global_keys, global_values, out_grad, query_gain, doc_start):
    rows = queries.shape[1]
    device = lax.axis_index("ctx")
    q, do = queries[0], out_grad[0]
    gain = query_gain[None]
    keys, values = [global_keys[0]], [global_values[0]]
    for _ in range(1, REACH):
        keys.insert(0, shifted(keys[0], "ctx", 1))
    for _ in range(1, REACH):
        values.insert(0, shifted(values[0], "ctx", 1))
    lo = doc_start[0] * BLOCK - (device - (REACH - 1)) * rows
    probs, *dv = attention_probs(lo, q, do, gain, keys)
    attn_out, query_grad, gain_term, *dk = attention_grads(q, do, gain, probs, keys, values)
    value_total = dv[0]
    for part in dv[1:]:
        value_total = shifted(value_total, "ctx", -1) + part
    key_total = dk[0]
    for part in dk[1:]:
        key_total = shifted(key_total, "ctx", -1) + part
    gain_grad = all_sum(all_sum(gain_term[0], "dp"), "ctx")
    return (
        attn_out[None],
        query_grad[None],
        key_total.astype(jnp.bfloat16)[None],
        value_total.astype(jnp.bfloat16)[None],
        gain_grad,
    )


def solution(mesh):
    rows = P("dp", "ctx", None)
    return jax.shard_map(
        local,
        mesh=mesh,
        in_specs=(rows, rows, rows, rows, P(), P("dp", "ctx")),
        out_specs=(rows, rows, rows, rows, P()),
        check_vma=False,
    )
```

```python
import functools
import math

import jax
import jax.numpy as jnp
from jax import lax
from jax.experimental import pallas as pl
from jax.experimental.pallas import tpu as pltpu
from jax.sharding import PartitionSpec as P


HD = 128
BLOCK = 128
REACH = 4
LOG2E = 1.4426950408889634
SCALE_STEPS = 64.0
SCALE_ROWS = 16
CODE_MAX = 32767.0
CODE_ROWS = HD + SCALE_ROWS


def shifted(value, steps):
    count = lax.axis_size("ctx")
    first, last = (max(0, -steps), min(count, count - steps))
    pairs = [(source, source + steps) for source in range(first, last)]
    return lax.ppermute(value, "ctx", pairs)


def exchange(value, axis, first, second):
    count = math.prod(lax.axis_size(a) for a in axis)
    one, two, three = (
        lax.ppermute(value, axis, [(i, i ^ bits) for i in range(count)])
        for bits in (first, second, first | second)
    )
    return (value + one) + (two + three)


def encode(value):
    top = jnp.maximum(jnp.max(jnp.abs(value), axis=0, keepdims=True), 2.0**-100)
    level = jnp.ceil(jnp.log2(top) * SCALE_STEPS)
    coded = jnp.round(value * (jnp.exp2(level * (-1.0 / SCALE_STEPS)) * CODE_MAX))
    level = jnp.broadcast_to(level, (SCALE_ROWS, value.shape[1]))
    return tuple(v.astype(jnp.int32).astype(jnp.int16) for v in (coded, level))


def decode(coded, level):
    level = level.astype(jnp.int32).astype(jnp.float32)[:1]
    return coded.astype(jnp.int32).astype(jnp.float32) * (
        jnp.exp2(level * (1.0 / SCALE_STEPS)) * (1.0 / CODE_MAX)
    )


def dot(a, b, dims=((1,), (0,))):
    return lax.dot_general(a, b, (dims, ((), ())), preferred_element_type=jnp.float32)


def probs_kernel(group, rows, lo, q_ref, g_ref, gain_ref, *refs):
    k_refs, (p_ref, *dv_refs) = refs[:REACH], refs[REACH : 2 * REACH + 1]
    bias, k_all, p_low, g_all = refs[2 * REACH + 1 :]
    width = REACH * rows

    @pl.when(pl.program_id(0) == 0)
    def _():
        key = lax.broadcasted_iota(jnp.int32, (width, rows), 0)
        query = lax.broadcasted_iota(jnp.int32, (width, rows), 1)
        begin = jnp.where(query < BLOCK, lo[0], lo[1])
        allowed = (key >= begin) & (key <= query + (width - rows))
        bias[...] = jnp.where(allowed, 0.0, -jnp.inf)

    for j in range(REACH):
        k_all[j * rows : (j + 1) * rows, :] = k_refs[j][...]
    for g in range(group):
        cols = slice(g * HD, (g + 1) * HD)
        g_all[g * rows : (g + 1) * rows, :] = g_ref[:, cols]
        scaled = (q_ref[:, cols].astype(jnp.float32) * gain_ref[:, cols]).astype(jnp.bfloat16)
        raw = dot(k_all[...], scaled, ((1,), (1,))) + bias[...]
        top = jnp.max(raw, axis=0, keepdims=True)
        e = jnp.exp2((raw - top) * (LOG2E / math.sqrt(HD)))
        probs = e * (1.0 / jnp.sum(e, axis=0, keepdims=True))
        p_ref[g] = probs
        p_low[:, g * rows : (g + 1) * rows] = probs.astype(jnp.bfloat16)
    dv = dot(p_low[...], g_all[...])
    dv_refs[0][:HD, :], dv_refs[0][HD:, :] = encode(dv[:rows, :].T)
    for j in range(1, REACH):
        dv_refs[j][...] = dv[j * rows : (j + 1) * rows, :].T


def grads_kernel(group, rows, skip, q_ref, g_ref, gain_ref, p_ref, *refs):
    k_refs, v_refs = refs[:REACH], refs[REACH : 2 * REACH]
    refs = refs[: 2 * REACH] + refs[2 * REACH + skip :]
    o_ref, dq_ref, gain_out, *dk_refs = refs[2 * REACH : 3 * REACH + 3]
    k_t, v_t, v_all, ds_all, q_all = refs[3 * REACH + 3 :]
    factor = 1.0 / math.sqrt(HD)
    for j in range(REACH):
        part = slice(j * rows, (j + 1) * rows)
        v_all[part, :] = v_refs[j][...]
        k_t[:, part] = k_refs[j][...].T
        v_t[:, part] = v_refs[j][...].T
    for g in range(group):
        cols = slice(g * HD, (g + 1) * HD)
        q32 = q_ref[:, cols].astype(jnp.float32)
        gain = gain_ref[:, cols]
        q_all[g * rows : (g + 1) * rows, :] = (q32 * gain).astype(jnp.bfloat16)
        probs = p_ref[g]
        out_t = dot(v_t[...], probs.astype(jnp.bfloat16)).astype(jnp.bfloat16)
        o_ref[:, cols] = out_t.T
        g_t = g_ref[:, cols].T
        delta = jnp.sum(g_t.astype(jnp.float32) * out_t.astype(jnp.float32), axis=0, keepdims=True)
        ds = (probs * (dot(v_all[...], g_t) - delta)).astype(jnp.bfloat16)
        ds_all[:, g * rows : (g + 1) * rows] = ds
        dscaled = (dot(k_t[...], ds) * factor).T
        dq_ref[:, cols] = (dscaled * gain).astype(jnp.bfloat16)
        gain_out[:, cols] = jnp.sum(dscaled * q32, axis=0, keepdims=True)
    dk = dot(ds_all[...], q_all[...]) * factor
    dk_refs[0][:HD, :], dk_refs[0][HD:, :] = encode(dk[:rows, :].T)
    for j in range(1, REACH):
        dk_refs[j][...] = dk[j * rows : (j + 1) * rows, :].T


def hop_kernel(kv_count, last, message, part, out):
    for c in range(kv_count):
        at, here = c * CODE_ROWS, slice(c * HD, (c + 1) * HD)
        total = part[here, :] + decode(
            message[at : at + HD, :], message[at + HD : at + CODE_ROWS, :]
        )
        if last:
            out[:, here] = total.T.astype(jnp.bfloat16)
        else:
            out[at : at + HD, :], out[at + HD : at + CODE_ROWS, :] = encode(total)


def hop(message, part, last):
    kv_channels, rows = part.shape
    shape = jax.ShapeDtypeStruct((rows, kv_channels), jnp.bfloat16) if last else message
    return pl.pallas_call(
        functools.partial(hop_kernel, kv_channels // HD, last),
        out_shape=jax.ShapeDtypeStruct(shape.shape, shape.dtype),
        compiler_params=pltpu.CompilerParams(vmem_limit_bytes=16 * 2**20),
        cost_estimate=pl.CostEstimate(
            flops=10 * part.size, bytes_accessed=8 * part.size, transcendentals=0
        ),
        name="last_hop" if last else "hop",
    )(message, part)


def attention_probs(lo, queries, out_grad, gain, keys):
    rows, channels = queries.shape
    kv_channels = keys[0].shape[1]
    kv_count = kv_channels // HD
    group = channels // kv_channels
    width = REACH * rows
    wide = pl.BlockSpec((rows, group * HD), lambda c, lo: (0, c))
    thin = pl.BlockSpec((rows, HD), lambda c, lo: (0, c))
    code = pl.BlockSpec((CODE_ROWS, rows), lambda c, lo: (c, 0))
    part = pl.BlockSpec((HD, rows), lambda c, lo: (c, 0))
    return pl.pallas_call(
        functools.partial(probs_kernel, group, rows),
        out_shape=[jax.ShapeDtypeStruct((kv_count * group, width, rows), jnp.float32)]
        + [jax.ShapeDtypeStruct((kv_count * CODE_ROWS, rows), jnp.int16)]
        + [jax.ShapeDtypeStruct((kv_channels, rows), jnp.float32)] * (REACH - 1),
        grid_spec=pltpu.PrefetchScalarGridSpec(
            num_scalar_prefetch=1,
            grid=(kv_count,),
            in_specs=[wide, wide, pl.BlockSpec((1, group * HD), lambda c, lo: (0, c))]
            + [thin] * REACH,
            out_specs=[pl.BlockSpec((group, width, rows), lambda c, lo: (c, 0, 0)), code]
            + [part] * (REACH - 1),
            scratch_shapes=[
                pltpu.VMEM((width, rows), jnp.float32),
                pltpu.VMEM((width, HD), jnp.bfloat16),
                pltpu.VMEM((width, group * rows), jnp.bfloat16),
                pltpu.VMEM((group * rows, HD), jnp.bfloat16),
            ],
        ),
        cost_estimate=pl.CostEstimate(
            flops=4 * kv_count * group * width * rows * HD,
            bytes_accessed=4 * kv_count * group * width * rows,
            transcendentals=kv_count * group * width * rows,
        ),
        name="probs",
    )(lo, queries, out_grad, gain, *keys)


def attention_grads(first, count, before, queries, out_grad, gain, probs, keys, values):
    rows, channels = queries.shape
    kv_channels = keys[0].shape[1]
    kv_count = kv_channels // HD
    group = channels // kv_channels
    width = REACH * rows
    wide = pl.BlockSpec((rows, group * HD), lambda c: (0, c + first))
    line = pl.BlockSpec((1, group * HD), lambda c: (0, c + first))
    thin = pl.BlockSpec((rows, HD), lambda c: (0, c + first))
    code = pl.BlockSpec((CODE_ROWS, rows), lambda c: (c + first, 0))
    part = pl.BlockSpec((HD, rows), lambda c: (c + first, 0))
    n_in = 4 + 2 * REACH
    return pl.pallas_call(
        functools.partial(grads_kernel, group, rows, len(before)),
        out_shape=[jax.ShapeDtypeStruct((rows, channels), jnp.bfloat16)] * 2
        + [jax.ShapeDtypeStruct((1, channels), jnp.float32)]
        + [jax.ShapeDtypeStruct((kv_count * CODE_ROWS, rows), jnp.int16)]
        + [jax.ShapeDtypeStruct((kv_channels, rows), jnp.float32)] * (REACH - 1),
        grid=(count,),
        in_specs=[wide, wide, line]
        + [pl.BlockSpec((group, width, rows), lambda c: (c + first, 0, 0))]
        + [thin] * (2 * REACH)
        + [pl.BlockSpec(memory_space=pl.ANY)] * len(before),
        out_specs=[wide, wide, line, code] + [part] * (REACH - 1),
        scratch_shapes=[
            pltpu.VMEM((HD, width), jnp.bfloat16),
            pltpu.VMEM((HD, width), jnp.bfloat16),
            pltpu.VMEM((width, HD), jnp.bfloat16),
            pltpu.VMEM((width, group * rows), jnp.bfloat16),
            pltpu.VMEM((group * rows, HD), jnp.bfloat16),
        ],
        input_output_aliases={n_in + i: i for i in range(len(before))},
        cost_estimate=pl.CostEstimate(
            flops=8 * count * group * width * rows * HD,
            bytes_accessed=4 * count * group * width * rows,
            transcendentals=0,
        ),
    )(queries, out_grad, gain, probs, *keys, *values, *before)


def step(queries, global_keys, global_values, out_grad, query_gain, doc_start):
    rows = queries.shape[1]
    device = lax.axis_index("ctx")
    q, do = queries[0], out_grad[0]
    gain = query_gain[None]
    together = lax.optimization_barrier
    keys, values = [global_keys[0]], [global_values[0]]
    for _ in range(1, REACH):
        keys.insert(0, shifted(keys[0], 1))
    for _ in range(1, REACH - 1):
        values.insert(0, shifted(values[0], 1))
    keys[0], values[0] = together((keys[0], values[0]))
    values.insert(0, shifted(values[0], 1))
    lo = doc_start[0] * BLOCK - (device - (REACH - 1)) * rows
    half = keys[0].shape[1] // HD // 2

    probs, dv_sum, *dv = attention_probs(lo, q, do, gain, keys)
    moved = shifted(dv_sum, -1)
    early = attention_grads(0, half, [], q, do, gain, probs, keys, values)
    moved, gain = together((moved, gain))
    moved = shifted(hop(moved, dv[0], False), -1)
    attn_out, query_grad, gain_term, dk_sum, *dk = attention_grads(
        half, half, early, q, do, gain, probs, keys, values
    )
    moved, dk_sum = together((moved, dk_sum))
    dk_moved = shifted(dk_sum, -1)
    moved = shifted(hop(moved, dv[1], False), -1)
    both = ("dp", "ctx")
    total = exchange(gain_term[0], both, 64, 128)
    total = exchange(total, both, 8, 16)
    dk_moved, moved, total = together((dk_moved, moved, total))
    dk_moved = shifted(hop(dk_moved, dk[0], False), -1)
    value_grad = hop(moved, dv[2], True)
    total = exchange(total, both, 1, 2)
    dk_moved, total = together((dk_moved, total))
    dk_moved = shifted(hop(dk_moved, dk[1], False), -1)
    gain_grad = exchange(total, both, 4, 32)
    key_grad = hop(dk_moved, dk[2], True)
    return (
        attn_out[None],
        query_grad[None],
        key_grad[None],
        value_grad[None],
        gain_grad,
    )


def solution(mesh):
    rows = P("dp", "ctx", None)
    return jax.shard_map(
        step,
        mesh=mesh,
        in_specs=(rows, rows, rows, rows, P(), P("dp", "ctx")),
        out_specs=(rows, rows, rows, rows, P()),
        check_vma=False,
    )
```

```python
import functools
import math

import jax
import jax.numpy as jnp
from jax import lax
from jax.experimental import pallas as pl
from jax.experimental.pallas import tpu as pltpu
from jax.sharding import PartitionSpec as P


HD = 128
BLOCK = 128
REACH = 4
EXPONENT = 1.4426950408889634 / math.sqrt(HD)
SCALE_STEPS = 64.0
SCALE_ROWS = 16
CODE_MAX = 32767.0
CODE_ROWS = HD + SCALE_ROWS


def shifted(value, steps):
    count = lax.axis_size("ctx")
    first, last = (max(0, -steps), min(count, count - steps))
    pairs = [(source, source + steps) for source in range(first, last)]
    return lax.ppermute(value, "ctx", pairs)


def exchange(value, axis, first, second):
    count = math.prod(lax.axis_size(a) for a in axis)
    one, two, three = (
        lax.ppermute(value, axis, [(i, i ^ bits) for i in range(count)])
        for bits in (first, second, first | second)
    )
    return (value + one) + (two + three)


def encode(value):
    top = jnp.maximum(jnp.max(jnp.abs(value), axis=0, keepdims=True), 2.0**-100)
    level = jnp.ceil(jnp.log2(top) * SCALE_STEPS)
    coded = jnp.round(value * (jnp.exp2(level * (-1.0 / SCALE_STEPS)) * CODE_MAX))
    level = jnp.broadcast_to(level, (SCALE_ROWS, value.shape[1]))
    return tuple(v.astype(jnp.int32).astype(jnp.int16) for v in (coded, level))


def decode(coded, level):
    level = level.astype(jnp.int32).astype(jnp.float32)[:1]
    return coded.astype(jnp.int32).astype(jnp.float32) * (
        jnp.exp2(level * (1.0 / SCALE_STEPS)) * (1.0 / CODE_MAX)
    )


def dot(a, b, dims=((1,), (0,))):
    return lax.dot_general(a, b, (dims, ((), ())), preferred_element_type=jnp.float32)


def softened(raw):
    top = jnp.max(raw, axis=0, keepdims=True)
    e = jnp.exp2((raw - top) * EXPONENT)
    return e, top, jnp.sum(e, axis=0, keepdims=True)


def scaled_query(q_ref, gain_ref, cols):
    return (q_ref[:, cols].astype(jnp.float32) * gain_ref[:, cols]).astype(jnp.bfloat16)


def scores_kernel(group, own, q_ref, gain_ref, k_ref, e_ref, top_ref, sum_ref):
    rows = k_ref.shape[0]
    per = rows // BLOCK
    if own:
        key = lax.broadcasted_iota(jnp.int32, (BLOCK, rows), 0)
        query = lax.broadcasted_iota(jnp.int32, (BLOCK, rows), 1)
    for g in range(group):
        scaled = scaled_query(q_ref, gain_ref, slice(g * HD, (g + 1) * HD))
        for b in range(per):
            here = slice(b * BLOCK, (b + 1) * BLOCK)
            raw = dot(k_ref[here, :], scaled, ((1,), (1,)))
            if own:
                later = (key + b * BLOCK > query) & (query >= b * BLOCK)
                raw = jnp.where(later, -jnp.inf, raw)
            e, top, total = softened(raw)
            at = slice(g * per + b, g * per + b + 1)
            e_ref[g, here, :], top_ref[0, at, :], sum_ref[0, at, :] = e, top, total


def far_kernel(group, lo, q_ref, g_ref, gain_ref, k_ref, *refs):
    stats = refs[: 2 * (REACH - 1)]
    e_ref, w_ref, dv_ref, p_low, g_all = refs[2 * (REACH - 1) :]
    rows = k_ref.shape[0]
    per = rows // BLOCK
    blocks = REACH * per
    half = lax.broadcasted_iota(jnp.int32, (1, rows), 1) // BLOCK
    begin = jnp.where(half == 0, lo[0], lo[1])
    allowed = [
        (begin <= b * BLOCK) & (half >= b - (REACH - 1) * per) for b in range(blocks)
    ]
    for g in range(group):
        cols = slice(g * HD, (g + 1) * HD)
        g_all[g * rows : (g + 1) * rows, :] = g_ref[:, cols]
        scaled = scaled_query(q_ref, gain_ref, cols)
        tops, sums = [], []
        for b in range(per):
            here = slice(b * BLOCK, (b + 1) * BLOCK)
            e, top, total = softened(dot(k_ref[here, :], scaled, ((1,), (1,))))
            e_ref[g, here, :] = e
            tops.append(top)
            sums.append(total)
        for j in range(REACH - 1):
            for b in range(per):
                at = slice(g * per + b, g * per + b + 1)
                tops.append(stats[2 * j][0, at, :])
                sums.append(stats[2 * j + 1][0, at, :])
        tops = [jnp.where(ok, top, -jnp.inf) for ok, top in zip(allowed, tops, strict=True)]
        highest = functools.reduce(jnp.maximum, tops)
        shares = [jnp.exp2((top - highest) * EXPONENT) for top in tops]
        total = sum(share * part for share, part in zip(shares, sums, strict=True))
        inverse = 1.0 / total
        for b in range(blocks):
            weight = shares[b] * inverse
            w_ref[0, g * blocks + b : g * blocks + b + 1, :] = weight
            if b < per:
                here = slice(b * BLOCK, (b + 1) * BLOCK)
                p_low[here, g * rows : (g + 1) * rows] = (e_ref[g, here, :] * weight).astype(
                    jnp.bfloat16
                )
    dv_ref[:HD, :], dv_ref[HD:, :] = encode(dot(p_low[...], g_all[...]).T)


def values_kernel(group, g_ref, w_ref, *refs):
    e_refs, dv_refs = refs[: REACH - 1], refs[REACH - 1 : 2 * (REACH - 1)]
    p_low, g_all = refs[2 * (REACH - 1) :]
    rows = g_ref.shape[0]
    per = rows // BLOCK
    blocks = REACH * per
    for g in range(group):
        g_all[g * rows : (g + 1) * rows, :] = g_ref[:, g * HD : (g + 1) * HD]
        for j in range(REACH - 1):
            for b in range(per):
                here = slice(b * BLOCK, (b + 1) * BLOCK)
                at = g * blocks + (j + 1) * per + b
                probs = e_refs[j][g, here, :] * w_ref[0, at : at + 1, :]
                there = slice(j * rows + b * BLOCK, j * rows + (b + 1) * BLOCK)
                p_low[there, g * rows : (g + 1) * rows] = probs.astype(jnp.bfloat16)
    dv = dot(p_low[...], g_all[...])
    for j in range(REACH - 1):
        dv_refs[j][...] = dv[j * rows : (j + 1) * rows, :].T


def grads_kernel(group, rows, skip, q_ref, g_ref, gain_ref, w_ref, *refs):
    e_refs, k_refs, v_refs = (refs[i * REACH : (i + 1) * REACH] for i in range(3))
    refs = refs[3 * REACH + skip :]
    o_ref, dq_ref, gain_out, *dk_refs = refs[: REACH + 3]
    k_t, v_t, v_all, p_all, ds_all, q_all = refs[REACH + 3 :]
    per = rows // BLOCK
    blocks = REACH * per
    factor = 1.0 / math.sqrt(HD)
    for j in range(REACH):
        part = slice(j * rows, (j + 1) * rows)
        v_all[part, :] = v_refs[j][...]
        k_t[:, part] = k_refs[j][...].T
        v_t[:, part] = v_refs[j][...].T

    def probs_of(g, b):
        here = slice(b % per * BLOCK, (b % per + 1) * BLOCK)
        at = g * blocks + b
        return e_refs[b // per][g, here, :] * w_ref[0, at : at + 1, :]

    for g in range(group):
        cols = slice(g * HD, (g + 1) * HD)
        mine = slice(g * rows, (g + 1) * rows)
        q32 = q_ref[:, cols].astype(jnp.float32)
        gain = gain_ref[:, cols]
        q_all[mine, :] = (q32 * gain).astype(jnp.bfloat16)
        for b in range(blocks):
            p_all[g % 2, b * BLOCK : (b + 1) * BLOCK, :] = probs_of(g, b).astype(jnp.bfloat16)
        out_t = dot(v_t[...], p_all[g % 2]).astype(jnp.bfloat16)
        o_ref[:, cols] = out_t.T
        g_t = g_ref[:, cols].T
        delta = jnp.sum(g_t.astype(jnp.float32) * out_t.astype(jnp.float32), axis=0, keepdims=True)
        for b in range(blocks):
            here = slice(b * BLOCK, (b + 1) * BLOCK)
            ds = probs_of(g, b) * (dot(v_all[here, :], g_t) - delta)
            ds_all[here, mine] = ds.astype(jnp.bfloat16)
        dscaled = (dot(k_t[...], ds_all[:, mine]) * factor).T
        dq_ref[:, cols] = (dscaled * gain).astype(jnp.bfloat16)
        gain_out[:, cols] = jnp.sum(dscaled * q32, axis=0, keepdims=True)
    dk = dot(ds_all[...], q_all[...]) * factor
    dk_refs[0][:HD, :], dk_refs[0][HD:, :] = encode(dk[:rows, :].T)
    for j in range(1, REACH):
        dk_refs[j][...] = dk[j * rows : (j + 1) * rows, :].T


def hop_kernel(kv_count, last, message, part, out):
    for c in range(kv_count):
        at, here = c * CODE_ROWS, slice(c * HD, (c + 1) * HD)
        total = part[here, :] + decode(
            message[at : at + HD, :], message[at + HD : at + CODE_ROWS, :]
        )
        if last:
            out[:, here] = total.T.astype(jnp.bfloat16)
        else:
            out[at : at + HD, :], out[at + HD : at + CODE_ROWS, :] = encode(total)


def hop(message, part, last):
    kv_channels, rows = part.shape
    shape = jax.ShapeDtypeStruct((rows, kv_channels), jnp.bfloat16) if last else message
    return pl.pallas_call(
        functools.partial(hop_kernel, kv_channels // HD, last),
        out_shape=jax.ShapeDtypeStruct(shape.shape, shape.dtype),
        compiler_params=pltpu.CompilerParams(vmem_limit_bytes=16 * 2**20),
        cost_estimate=pl.CostEstimate(
            flops=10 * part.size, bytes_accessed=8 * part.size, transcendentals=0
        ),
        name="last_hop" if last else "hop",
    )(message, part)


class Shapes:
    def __init__(self, queries, keys, first=0):
        self.rows, self.channels = queries.shape
        self.kv_channels = keys.shape[1]
        self.kv_count = self.kv_channels // HD
        self.group = self.channels // self.kv_channels
        self.blocks = REACH * self.rows // BLOCK
        self.stat_rows = self.group * self.rows // BLOCK
        rows, group = self.rows, self.group
        self.wide = pl.BlockSpec((rows, group * HD), lambda c, *_: (0, c + first))
        self.line = pl.BlockSpec((1, group * HD), lambda c, *_: (0, c + first))
        self.thin = pl.BlockSpec((rows, HD), lambda c, *_: (0, c + first))
        self.code = pl.BlockSpec((CODE_ROWS, rows), lambda c, *_: (c + first, 0))
        self.part = pl.BlockSpec((HD, rows), lambda c, *_: (c + first, 0))
        self.heads = pl.BlockSpec((group, rows, rows), lambda c, *_: (c + first, 0, 0))
        self.stat = pl.BlockSpec((1, self.stat_rows, rows), lambda c, *_: (c + first, 0, 0))
        self.weight = pl.BlockSpec(
            (1, group * self.blocks, rows), lambda c, *_: (c + first, 0, 0)
        )

    def array(self, dtype, *shape):
        return jax.ShapeDtypeStruct(shape, dtype)

    def heads_array(self):
        return self.array(jnp.float32, self.kv_count * self.group, self.rows, self.rows)

    def stat_array(self):
        return self.array(jnp.float32, self.kv_count, self.stat_rows, self.rows)

    def weight_array(self):
        return self.array(jnp.float32, self.kv_count, self.group * self.blocks, self.rows)

    def code_array(self):
        return self.array(jnp.int16, self.kv_count * CODE_ROWS, self.rows)

    def part_array(self):
        return self.array(jnp.float32, self.kv_channels, self.rows)

    def cost(self, products, chunks, exps, count=None):
        heads = (self.kv_count if count is None else count) * self.group
        size = heads * chunks * self.rows * self.rows
        return pl.CostEstimate(
            flops=2 * products * size * HD, bytes_accessed=4 * size, transcendentals=exps * size
        )


def chunk_scores(queries, gain, keys, own):
    s = Shapes(queries, keys)
    return pl.pallas_call(
        functools.partial(scores_kernel, s.group, own),
        out_shape=[s.heads_array(), s.stat_array(), s.stat_array()],
        grid=(s.kv_count,),
        in_specs=[s.wide, s.line, s.thin],
        out_specs=[s.heads, s.stat, s.stat],
        cost_estimate=s.cost(1, 1, 1),
        name="scores_own" if own else "scores",
    )(queries, gain, keys)


def far_scores(lo, queries, out_grad, gain, keys, stats):
    s = Shapes(queries, keys)
    return pl.pallas_call(
        functools.partial(far_kernel, s.group),
        out_shape=[s.heads_array(), s.weight_array(), s.code_array()],
        grid_spec=pltpu.PrefetchScalarGridSpec(
            num_scalar_prefetch=1,
            grid=(s.kv_count,),
            in_specs=[s.wide, s.wide, s.line, s.thin] + [s.stat] * len(stats),
            out_specs=[s.heads, s.weight, s.code],
            scratch_shapes=[
                pltpu.VMEM((s.rows, s.group * s.rows), jnp.bfloat16),
                pltpu.VMEM((s.group * s.rows, HD), jnp.bfloat16),
            ],
        ),
        cost_estimate=s.cost(2, 1, 1),
        name="far_scores",
    )(lo, queries, out_grad, gain, keys, *stats)


def near_values(queries, keys, out_grad, weights, heads):
    s = Shapes(queries, keys)
    near = REACH - 1
    return pl.pallas_call(
        functools.partial(values_kernel, s.group),
        out_shape=[s.part_array()] * near,
        grid=(s.kv_count,),
        in_specs=[s.wide, s.weight] + [s.heads] * near,
        out_specs=[s.part] * near,
        scratch_shapes=[
            pltpu.VMEM((near * s.rows, s.group * s.rows), jnp.bfloat16),
            pltpu.VMEM((s.group * s.rows, HD), jnp.bfloat16),
        ],
        cost_estimate=s.cost(1, near, 0),
        name="near_values",
    )(out_grad, weights, *heads)


def attention_grads(first, count, before, queries, out_grad, gain, weights, heads, keys, values):
    s = Shapes(queries, keys[0], first)
    width = REACH * s.rows
    n_in = 4 + 3 * REACH
    return pl.pallas_call(
        functools.partial(grads_kernel, s.group, s.rows, len(before)),
        out_shape=[s.array(jnp.bfloat16, s.rows, s.channels)] * 2
        + [s.array(jnp.float32, 1, s.channels), s.code_array()]
        + [s.part_array()] * (REACH - 1),
        grid=(count,),
        in_specs=[s.wide, s.wide, s.line, s.weight]
        + [s.heads] * REACH
        + [s.thin] * (2 * REACH)
        + [pl.BlockSpec(memory_space=pl.ANY)] * len(before),
        out_specs=[s.wide, s.wide, s.line, s.code] + [s.part] * (REACH - 1),
        scratch_shapes=[
            pltpu.VMEM((HD, width), jnp.bfloat16),
            pltpu.VMEM((HD, width), jnp.bfloat16),
            pltpu.VMEM((width, HD), jnp.bfloat16),
            pltpu.VMEM((2, width, s.rows), jnp.bfloat16),
            pltpu.VMEM((width, s.group * s.rows), jnp.bfloat16),
            pltpu.VMEM((s.group * s.rows, HD), jnp.bfloat16),
        ],
        input_output_aliases={n_in + i: i for i in range(len(before))},
        cost_estimate=s.cost(4, REACH, 0, count),
    )(queries, out_grad, gain, weights, *heads, *keys, *values, *before)


def step(queries, global_keys, global_values, out_grad, query_gain, doc_start):
    rows = queries.shape[1]
    device = lax.axis_index("ctx")
    q, do = queries[0], out_grad[0]
    gain = query_gain[None]
    together = lax.optimization_barrier
    lo = doc_start[0] * BLOCK - (device - (REACH - 1)) * rows
    own_keys, own_values = global_keys[0], global_values[0]
    near = [chunk_scores(q, gain, own_keys, True)]
    keys, values = [own_keys], [own_values]
    for i in range(1, REACH):
        keys.insert(0, shifted(keys[0], 1))
        if i < REACH - 1:
            near.insert(0, chunk_scores(q, gain, keys[0], False))
            values.insert(0, shifted(values[0], 1))
    keys[0], values[0] = together((keys[0], values[0]))
    values.insert(0, shifted(values[0], 1))
    half = own_keys.shape[1] // HD // 2

    stats = [stat for _, *pair in near for stat in pair]
    far, weights, moved = far_scores(lo, q, do, gain, keys[0], stats)
    heads = [far] + [e for e, *_ in near]
    moved = shifted(moved, -1)
    dv = near_values(q, own_keys, do, weights, heads[1:])
    moved = shifted(hop(moved, dv[0], False), -1)
    early = attention_grads(0, half, [], q, do, gain, weights, heads, keys, values)
    moved = shifted(hop(moved, dv[1], False), -1)
    attn_out, query_grad, gain_term, dk_moved, *dk = attention_grads(
        half, half, early, q, do, gain, weights, heads, keys, values
    )
    dk_moved = shifted(dk_moved, -1)
    both = ("dp", "ctx")
    total = exchange(gain_term[0], both, 64, 128)
    value_grad = hop(moved, dv[2], True)
    dk_moved, total = together((dk_moved, total))
    dk_moved = shifted(hop(dk_moved, dk[0], False), -1)
    total = exchange(total, both, 8, 16)
    dk_moved, total = together((dk_moved, total))
    dk_moved = shifted(hop(dk_moved, dk[1], False), -1)
    total = exchange(total, both, 1, 2)
    gain_grad = exchange(total, both, 4, 32)
    key_grad = hop(dk_moved, dk[2], True)
    return (
        attn_out[None],
        query_grad[None],
        key_grad[None],
        value_grad[None],
        gain_grad,
    )


def solution(mesh):
    rows = P("dp", "ctx", None)
    return jax.shard_map(
        step,
        mesh=mesh,
        in_specs=(rows, rows, rows, rows, P(), P("dp", "ctx")),
        out_specs=(rows, rows, rows, rows, P()),
        check_vma=False,
    )
```

```python
import functools
import math

import jax
import jax.numpy as jnp
from jax import lax
from jax.experimental import pallas as pl
from jax.experimental.pallas import tpu as pltpu
from jax.sharding import PartitionSpec as P


HD = 128
BLOCK = 128
REACH = 4
Z_CHIPS = 8
EXPONENT = 1.4426950408889634 / math.sqrt(HD)
SCALE_STEPS = 64.0
SCALE_ROWS = 16
CODE_MAX = 32767.0
CODE_ROWS = HD + SCALE_ROWS


def shifted(value, steps):
    count = lax.axis_size("ctx")
    first, last = (max(0, -steps), min(count, count - steps))
    pairs = [(source, source + steps) for source in range(first, last)]
    return lax.ppermute(value, "ctx", pairs)


def gathered_sum(value, axis, size, groups=None):
    copies = jnp.broadcast_to(value[None], (size, *value.shape))
    parts = lax.all_to_all(copies, axis, 0, 0, tiled=True, axis_index_groups=groups)
    return jnp.sum(parts, axis=0)


def pair_sum(value, step):
    pairs = [(i, i ^ step) for i in range(lax.axis_size("ctx"))]
    return value + lax.ppermute(value, "ctx", pairs)


def encode(value):
    top = jnp.maximum(jnp.max(jnp.abs(value), axis=0, keepdims=True), 2.0**-100)
    level = jnp.ceil(jnp.log2(top) * SCALE_STEPS)
    coded = jnp.round(value * (jnp.exp2(level * (-1.0 / SCALE_STEPS)) * CODE_MAX))
    level = jnp.broadcast_to(level, (SCALE_ROWS, value.shape[1]))
    return tuple(v.astype(jnp.int32).astype(jnp.int16) for v in (coded, level))


def decode(coded, level):
    level = level.astype(jnp.int32).astype(jnp.float32)[:1]
    return coded.astype(jnp.int32).astype(jnp.float32) * (
        jnp.exp2(level * (1.0 / SCALE_STEPS)) * (1.0 / CODE_MAX)
    )


def dot(a, b, dims=((1,), (0,))):
    return lax.dot_general(a, b, (dims, ((), ())), preferred_element_type=jnp.float32)


def softened(raw):
    top = jnp.max(raw, axis=0, keepdims=True)
    e = jnp.exp2((raw - top) * EXPONENT)
    return e, top, jnp.sum(e, axis=0, keepdims=True)


def scaled_query(q_ref, gain_ref, cols):
    return (q_ref[:, cols].astype(jnp.float32) * gain_ref[:, cols]).astype(jnp.bfloat16)


def scores_kernel(group, own, q_ref, gain_ref, k_ref, e_ref, top_ref, sum_ref):
    rows = k_ref.shape[0]
    per = rows // BLOCK
    if own:
        key = lax.broadcasted_iota(jnp.int32, (BLOCK, rows), 0)
        query = lax.broadcasted_iota(jnp.int32, (BLOCK, rows), 1)
    for g in range(group):
        scaled = scaled_query(q_ref, gain_ref, slice(g * HD, (g + 1) * HD))
        for b in range(per):
            here = slice(b * BLOCK, (b + 1) * BLOCK)
            raw = dot(k_ref[here, :], scaled, ((1,), (1,)))
            if own:
                later = (key + b * BLOCK > query) & (query >= b * BLOCK)
                raw = jnp.where(later, -jnp.inf, raw)
            e, top, total = softened(raw)
            at = slice(g * per + b, g * per + b + 1)
            e_ref[g, here, :], top_ref[0, at, :], sum_ref[0, at, :] = e, top, total


def far_kernel(group, lo, q_ref, g_ref, gain_ref, k_ref, *refs):
    stats = refs[: 2 * (REACH - 1)]
    e_ref, w_ref, dv_ref, p_low, g_all = refs[2 * (REACH - 1) :]
    rows = k_ref.shape[0]
    per = rows // BLOCK
    blocks = REACH * per
    half = lax.broadcasted_iota(jnp.int32, (1, rows), 1) // BLOCK
    begin = jnp.where(half == 0, lo[0], lo[1])
    allowed = [
        (begin <= b * BLOCK) & (half >= b - (REACH - 1) * per) for b in range(blocks)
    ]
    for g in range(group):
        cols = slice(g * HD, (g + 1) * HD)
        g_all[g * rows : (g + 1) * rows, :] = g_ref[:, cols]
        scaled = scaled_query(q_ref, gain_ref, cols)
        tops, sums = [], []
        for b in range(per):
            here = slice(b * BLOCK, (b + 1) * BLOCK)
            e, top, total = softened(dot(k_ref[here, :], scaled, ((1,), (1,))))
            e_ref[g, here, :] = e
            tops.append(top)
            sums.append(total)
        for j in range(REACH - 1):
            for b in range(per):
                at = slice(g * per + b, g * per + b + 1)
                tops.append(stats[2 * j][0, at, :])
                sums.append(stats[2 * j + 1][0, at, :])
        tops = [jnp.where(ok, top, -jnp.inf) for ok, top in zip(allowed, tops, strict=True)]
        highest = functools.reduce(jnp.maximum, tops)
        shares = [jnp.exp2((top - highest) * EXPONENT) for top in tops]
        total = sum(share * part for share, part in zip(shares, sums, strict=True))
        inverse = 1.0 / total
        for b in range(blocks):
            weight = shares[b] * inverse
            w_ref[0, g * blocks + b : g * blocks + b + 1, :] = weight
            if b < per:
                here = slice(b * BLOCK, (b + 1) * BLOCK)
                p_low[here, g * rows : (g + 1) * rows] = (e_ref[g, here, :] * weight).astype(
                    jnp.bfloat16
                )
    dv_ref[:HD, :], dv_ref[HD:, :] = encode(dot(p_low[...], g_all[...]).T)


def values_kernel(group, g_ref, w_ref, *refs):
    e_refs, dv_refs = refs[: REACH - 1], refs[REACH - 1 : 2 * (REACH - 1)]
    p_low, g_all = refs[2 * (REACH - 1) :]
    rows = g_ref.shape[0]
    per = rows // BLOCK
    blocks = REACH * per
    for g in range(group):
        g_all[g * rows : (g + 1) * rows, :] = g_ref[:, g * HD : (g + 1) * HD]
        for j in range(REACH - 1):
            for b in range(per):
                here = slice(b * BLOCK, (b + 1) * BLOCK)
                at = g * blocks + (j + 1) * per + b
                probs = e_refs[j][g, here, :] * w_ref[0, at : at + 1, :]
                there = slice(j * rows + b * BLOCK, j * rows + (b + 1) * BLOCK)
                p_low[there, g * rows : (g + 1) * rows] = probs.astype(jnp.bfloat16)
    dv = dot(p_low[...], g_all[...])
    for j in range(REACH - 1):
        dv_refs[j][...] = dv[j * rows : (j + 1) * rows, :].T


def grads_kernel(group, rows, skip, q_ref, g_ref, gain_ref, w_ref, *refs):
    e_refs, k_refs, v_refs = (refs[i * REACH : (i + 1) * REACH] for i in range(3))
    refs = refs[3 * REACH + skip :]
    o_ref, dq_ref, gain_out, *dk_refs = refs[: REACH + 3]
    k_t, v_t, v_all, p_all, ds_all, q_all = refs[REACH + 3 :]
    per = rows // BLOCK
    blocks = REACH * per
    factor = 1.0 / math.sqrt(HD)
    for j in range(REACH):
        part = slice(j * rows, (j + 1) * rows)
        v_all[part, :] = v_refs[j][...]
        k_t[:, part] = k_refs[j][...].T
        v_t[:, part] = v_refs[j][...].T

    def probs_of(g, b):
        here = slice(b % per * BLOCK, (b % per + 1) * BLOCK)
        at = g * blocks + b
        return e_refs[b // per][g, here, :] * w_ref[0, at : at + 1, :]

    for g in range(group):
        cols = slice(g * HD, (g + 1) * HD)
        mine = slice(g * rows, (g + 1) * rows)
        q32 = q_ref[:, cols].astype(jnp.float32)
        gain = gain_ref[:, cols]
        q_all[mine, :] = (q32 * gain).astype(jnp.bfloat16)
        for b in range(blocks):
            p_all[g % 2, b * BLOCK : (b + 1) * BLOCK, :] = probs_of(g, b).astype(jnp.bfloat16)
        out_t = dot(v_t[...], p_all[g % 2]).astype(jnp.bfloat16)
        o_ref[:, cols] = out_t.T
        g_t = g_ref[:, cols].T
        delta = jnp.sum(g_t.astype(jnp.float32) * out_t.astype(jnp.float32), axis=0, keepdims=True)
        for b in range(blocks):
            here = slice(b * BLOCK, (b + 1) * BLOCK)
            ds = probs_of(g, b) * (dot(v_all[here, :], g_t) - delta)
            ds_all[here, mine] = ds.astype(jnp.bfloat16)
        dscaled = (dot(k_t[...], ds_all[:, mine]) * factor).T
        dq_ref[:, cols] = (dscaled * gain).astype(jnp.bfloat16)
        gain_out[:, cols] = jnp.sum(dscaled * q32, axis=0, keepdims=True)
    dk = dot(ds_all[...], q_all[...]) * factor
    dk_refs[0][:HD, :], dk_refs[0][HD:, :] = encode(dk[:rows, :].T)
    for j in range(1, REACH):
        dk_refs[j][...] = dk[j * rows : (j + 1) * rows, :].T


def hop_kernel(kv_count, last, message, part, out):
    for c in range(kv_count):
        at, here = c * CODE_ROWS, slice(c * HD, (c + 1) * HD)
        total = part[here, :] + decode(
            message[at : at + HD, :], message[at + HD : at + CODE_ROWS, :]
        )
        if last:
            out[:, here] = total.T.astype(jnp.bfloat16)
        else:
            out[at : at + HD, :], out[at + HD : at + CODE_ROWS, :] = encode(total)


def hop(message, part, last):
    kv_channels, rows = part.shape
    shape = jax.ShapeDtypeStruct((rows, kv_channels), jnp.bfloat16) if last else message
    return pl.pallas_call(
        functools.partial(hop_kernel, kv_channels // HD, last),
        out_shape=jax.ShapeDtypeStruct(shape.shape, shape.dtype),
        compiler_params=pltpu.CompilerParams(vmem_limit_bytes=16 * 2**20),
        cost_estimate=pl.CostEstimate(
            flops=10 * part.size, bytes_accessed=8 * part.size, transcendentals=0
        ),
        name="last_hop" if last else "hop",
    )(message, part)


class Shapes:
    def __init__(self, queries, keys, first=0):
        self.rows, self.channels = queries.shape
        self.kv_channels = keys.shape[1]
        self.kv_count = self.kv_channels // HD
        self.group = self.channels // self.kv_channels
        self.blocks = REACH * self.rows // BLOCK
        self.stat_rows = self.group * self.rows // BLOCK
        rows, group = self.rows, self.group
        self.wide = pl.BlockSpec((rows, group * HD), lambda c, *_: (0, c + first))
        self.line = pl.BlockSpec((1, group * HD), lambda c, *_: (0, c + first))
        self.thin = pl.BlockSpec((rows, HD), lambda c, *_: (0, c + first))
        self.code = pl.BlockSpec((CODE_ROWS, rows), lambda c, *_: (c + first, 0))
        self.part = pl.BlockSpec((HD, rows), lambda c, *_: (c + first, 0))
        self.heads = pl.BlockSpec((group, rows, rows), lambda c, *_: (c + first, 0, 0))
        self.stat = pl.BlockSpec((1, self.stat_rows, rows), lambda c, *_: (c + first, 0, 0))
        self.weight = pl.BlockSpec(
            (1, group * self.blocks, rows), lambda c, *_: (c + first, 0, 0)
        )

    def array(self, dtype, *shape):
        return jax.ShapeDtypeStruct(shape, dtype)

    def heads_array(self):
        return self.array(jnp.float32, self.kv_count * self.group, self.rows, self.rows)

    def stat_array(self):
        return self.array(jnp.float32, self.kv_count, self.stat_rows, self.rows)

    def weight_array(self):
        return self.array(jnp.float32, self.kv_count, self.group * self.blocks, self.rows)

    def code_array(self):
        return self.array(jnp.int16, self.kv_count * CODE_ROWS, self.rows)

    def part_array(self):
        return self.array(jnp.float32, self.kv_channels, self.rows)

    def cost(self, products, chunks, exps, count=None):
        heads = (self.kv_count if count is None else count) * self.group
        size = heads * chunks * self.rows * self.rows
        return pl.CostEstimate(
            flops=2 * products * size * HD, bytes_accessed=4 * size, transcendentals=exps * size
        )


def chunk_scores(queries, gain, keys, own):
    s = Shapes(queries, keys)
    return pl.pallas_call(
        functools.partial(scores_kernel, s.group, own),
        out_shape=[s.heads_array(), s.stat_array(), s.stat_array()],
        grid=(s.kv_count,),
        in_specs=[s.wide, s.line, s.thin],
        out_specs=[s.heads, s.stat, s.stat],
        compiler_params=pltpu.CompilerParams(vmem_limit_bytes=8 * 2**20),
        cost_estimate=s.cost(1, 1, 1),
        name="scores_own" if own else "scores",
    )(queries, gain, keys)


def far_scores(lo, queries, out_grad, gain, keys, stats):
    s = Shapes(queries, keys)
    return pl.pallas_call(
        functools.partial(far_kernel, s.group),
        out_shape=[s.heads_array(), s.weight_array(), s.code_array()],
        grid_spec=pltpu.PrefetchScalarGridSpec(
            num_scalar_prefetch=1,
            grid=(s.kv_count,),
            in_specs=[s.wide, s.wide, s.line, s.thin] + [s.stat] * len(stats),
            out_specs=[s.heads, s.weight, s.code],
            scratch_shapes=[
                pltpu.VMEM((s.rows, s.group * s.rows), jnp.bfloat16),
                pltpu.VMEM((s.group * s.rows, HD), jnp.bfloat16),
            ],
        ),
        compiler_params=pltpu.CompilerParams(vmem_limit_bytes=16 * 2**20),
        cost_estimate=s.cost(2, 1, 1),
        name="far_scores",
    )(lo, queries, out_grad, gain, keys, *stats)


def near_values(queries, keys, out_grad, weights, heads):
    s = Shapes(queries, keys)
    near = REACH - 1
    return pl.pallas_call(
        functools.partial(values_kernel, s.group),
        out_shape=[s.part_array()] * near,
        grid=(s.kv_count,),
        in_specs=[s.wide, s.weight] + [s.heads] * near,
        out_specs=[s.part] * near,
        scratch_shapes=[
            pltpu.VMEM((near * s.rows, s.group * s.rows), jnp.bfloat16),
            pltpu.VMEM((s.group * s.rows, HD), jnp.bfloat16),
        ],
        compiler_params=pltpu.CompilerParams(vmem_limit_bytes=15 * 2**20),
        cost_estimate=s.cost(1, near, 0),
        name="near_values",
    )(out_grad, weights, *heads)


def attention_grads(first, count, before, queries, out_grad, gain, weights, heads, keys, values):
    s = Shapes(queries, keys[0], first)
    width = REACH * s.rows
    n_in = 4 + 3 * REACH
    return pl.pallas_call(
        functools.partial(grads_kernel, s.group, s.rows, len(before)),
        out_shape=[s.array(jnp.bfloat16, s.rows, s.channels)] * 2
        + [s.array(jnp.float32, 1, s.channels), s.code_array()]
        + [s.part_array()] * (REACH - 1),
        grid=(count,),
        in_specs=[s.wide, s.wide, s.line, s.weight]
        + [s.heads] * REACH
        + [s.thin] * (2 * REACH)
        + [pl.BlockSpec(memory_space=pl.ANY)] * len(before),
        out_specs=[s.wide, s.wide, s.line, s.code] + [s.part] * (REACH - 1),
        scratch_shapes=[
            pltpu.VMEM((HD, width), jnp.bfloat16),
            pltpu.VMEM((HD, width), jnp.bfloat16),
            pltpu.VMEM((width, HD), jnp.bfloat16),
            pltpu.VMEM((2, width, s.rows), jnp.bfloat16),
            pltpu.VMEM((width, s.group * s.rows), jnp.bfloat16),
            pltpu.VMEM((s.group * s.rows, HD), jnp.bfloat16),
        ],
        input_output_aliases={n_in + i: i for i in range(len(before))},
        compiler_params=pltpu.CompilerParams(vmem_limit_bytes=20 * 2**20),
        cost_estimate=s.cost(4, REACH, 0, count),
    )(queries, out_grad, gain, weights, *heads, *keys, *values, *before)


def step(queries, global_keys, global_values, out_grad, query_gain, doc_start):
    rows = queries.shape[1]
    device = lax.axis_index("ctx")
    q, do = queries[0], out_grad[0]
    gain = query_gain[None]
    together = lax.optimization_barrier
    lo = doc_start[0] * BLOCK - (device - (REACH - 1)) * rows
    lo, gain = together((lo, gain))
    own_keys, own_values = global_keys[0], global_values[0]
    near = [chunk_scores(q, gain, own_keys, True)]
    keys, values = [own_keys], [own_values]
    for i in range(1, REACH):
        keys.insert(0, shifted(keys[0], 1))
        if i < REACH - 1:
            near.insert(0, chunk_scores(q, gain, keys[0], False))
            values.insert(0, shifted(values[0], 1))
    values.insert(0, shifted(values[0], 1))
    half = own_keys.shape[1] // HD // 2

    stats = [stat for _, *pair in near for stat in pair]
    far, weights, moved = far_scores(lo, q, do, gain, keys[0], stats)
    heads = [far] + [e for e, *_ in near]
    moved = shifted(moved, -1)
    dv = near_values(q, own_keys, do, weights, heads[1:])
    moved = shifted(hop(moved, dv[0], False), -1)
    early = attention_grads(0, half, [], q, do, gain, weights, heads, keys, values)
    moved = shifted(hop(moved, dv[1], False), -1)
    attn_out, query_grad, gain_term, dk_moved, *dk = attention_grads(
        half, half, early, q, do, gain, weights, heads, keys, values
    )
    dk_moved = shifted(dk_moved, -1)
    count = lax.axis_size("ctx")
    columns = [[i + z for i in range(0, count, Z_CHIPS)] for z in range(Z_CHIPS)]
    total = gathered_sum(gain_term, "dp", lax.axis_size("dp"))
    value_grad = hop(moved, dv[2], True)
    dk_moved, total = together((dk_moved, total))
    dk_moved = shifted(hop(dk_moved, dk[0], False), -1)
    total = gathered_sum(total, "ctx", count // Z_CHIPS, columns)
    dk_moved, total = together((dk_moved, total))
    dk_moved = shifted(hop(dk_moved, dk[1], False), -1)
    total = pair_sum(total, 1)
    total = pair_sum(total, 2)
    gain_grad = pair_sum(total, 4)
    key_grad = hop(dk_moved, dk[2], True)
    return (
        attn_out[None],
        query_grad[None],
        key_grad[None],
        value_grad[None],
        gain_grad[0],
    )


def solution(mesh):
    rows = P("dp", "ctx", None)
    return jax.shard_map(
        step,
        mesh=mesh,
        in_specs=(rows, rows, rows, rows, P(), P("dp", "ctx")),
        out_specs=(rows, rows, rows, rows, P()),
        check_vma=False,
    )
```

```python
import functools
import math

import jax
import jax.numpy as jnp
from jax import lax
from jax.experimental import pallas as pl
from jax.experimental.pallas import tpu as pltpu
from jax.sharding import PartitionSpec as P


HD = 128
BLOCK = 128
REACH = 4
Z_CHIPS = 8
EXPONENT = 1.4426950408889634 / math.sqrt(HD)
SCALE_STEPS = 64.0
SCALE_ROWS = 16
CODE_MAX = 32767.0
CODE_ROWS = HD + SCALE_ROWS


def shifted(value, steps):
    count = lax.axis_size("ctx")
    first, last = (max(0, -steps), min(count, count - steps))
    pairs = [(source, source + steps) for source in range(first, last)]
    return lax.ppermute(value, "ctx", pairs)


def gathered_sum(value, axis, size, groups=None):
    copies = jnp.broadcast_to(value[None], (size, *value.shape))
    parts = lax.all_to_all(copies, axis, 0, 0, tiled=True, axis_index_groups=groups)
    return jnp.sum(parts, axis=0)


def pair_sum(value, step):
    pairs = [(i, i ^ step) for i in range(lax.axis_size("ctx"))]
    return value + lax.ppermute(value, "ctx", pairs)


def encode(value):
    top = jnp.maximum(jnp.max(jnp.abs(value), axis=0, keepdims=True), 2.0**-100)
    level = jnp.ceil(jnp.log2(top) * SCALE_STEPS)
    coded = jnp.round(value * (jnp.exp2(level * (-1.0 / SCALE_STEPS)) * CODE_MAX))
    level = jnp.broadcast_to(level, (SCALE_ROWS, value.shape[1]))
    return tuple(v.astype(jnp.int32).astype(jnp.int16) for v in (coded, level))


def decode(coded, level):
    level = level.astype(jnp.int32).astype(jnp.float32)[:1]
    return coded.astype(jnp.int32).astype(jnp.float32) * (
        jnp.exp2(level * (1.0 / SCALE_STEPS)) * (1.0 / CODE_MAX)
    )


def dot(a, b, dims=((1,), (0,))):
    return lax.dot_general(a, b, (dims, ((), ())), preferred_element_type=jnp.float32)


def softened(raw):
    top = jnp.max(raw, axis=0, keepdims=True)
    e = jnp.exp2((raw - top) * EXPONENT)
    return e, top, jnp.sum(e, axis=0, keepdims=True)


def scaled_query(q_ref, gain_ref, cols):
    return (q_ref[:, cols].astype(jnp.float32) * gain_ref[:, cols]).astype(jnp.bfloat16)


def scores_kernel(group, own, q_ref, gain_ref, k_ref, e_ref, top_ref, sum_ref):
    rows = k_ref.shape[0]
    per = rows // BLOCK
    if own:
        key = lax.broadcasted_iota(jnp.int32, (BLOCK, rows), 0)
        query = lax.broadcasted_iota(jnp.int32, (BLOCK, rows), 1)
    for g in range(group):
        scaled = scaled_query(q_ref, gain_ref, slice(g * HD, (g + 1) * HD))
        for b in range(per):
            here = slice(b * BLOCK, (b + 1) * BLOCK)
            raw = dot(k_ref[here, :], scaled, ((1,), (1,)))
            if own:
                later = (key + b * BLOCK > query) & (query >= b * BLOCK)
                raw = jnp.where(later, -jnp.inf, raw)
            e, top, total = softened(raw)
            at = slice(g * per + b, g * per + b + 1)
            e_ref[g, here, :], top_ref[0, at, :], sum_ref[0, at, :] = e, top, total


def far_kernel(group, lo, q_ref, g_ref, gain_ref, k_ref, *refs):
    stats = refs[: 2 * (REACH - 1)]
    e_ref, w_ref, dv_ref, p_low, g_all = refs[2 * (REACH - 1) :]
    rows = k_ref.shape[0]
    per = rows // BLOCK
    blocks = REACH * per
    half = lax.broadcasted_iota(jnp.int32, (1, rows), 1) // BLOCK
    begin = jnp.where(half == 0, lo[0], lo[1])
    allowed = [
        (begin <= b * BLOCK) & (half >= b - (REACH - 1) * per) for b in range(blocks)
    ]
    for g in range(group):
        cols = slice(g * HD, (g + 1) * HD)
        g_all[g * rows : (g + 1) * rows, :] = g_ref[:, cols]
        scaled = scaled_query(q_ref, gain_ref, cols)
        tops, sums = [], []
        for b in range(per):
            here = slice(b * BLOCK, (b + 1) * BLOCK)
            e, top, total = softened(dot(k_ref[here, :], scaled, ((1,), (1,))))
            e_ref[g, here, :] = e
            tops.append(top)
            sums.append(total)
        for j in range(REACH - 1):
            for b in range(per):
                at = slice(g * per + b, g * per + b + 1)
                tops.append(stats[2 * j][0, at, :])
                sums.append(stats[2 * j + 1][0, at, :])
        tops = [jnp.where(ok, top, -jnp.inf) for ok, top in zip(allowed, tops, strict=True)]
        highest = functools.reduce(jnp.maximum, tops)
        shares = [jnp.exp2((top - highest) * EXPONENT) for top in tops]
        total = sum(share * part for share, part in zip(shares, sums, strict=True))
        inverse = 1.0 / total
        for b in range(blocks):
            weight = shares[b] * inverse
            w_ref[0, g * blocks + b : g * blocks + b + 1, :] = weight
            if b < per:
                here = slice(b * BLOCK, (b + 1) * BLOCK)
                p_low[here, g * rows : (g + 1) * rows] = (e_ref[g, here, :] * weight).astype(
                    jnp.bfloat16
                )
    dv_ref[:HD, :], dv_ref[HD:, :] = encode(dot(p_low[...], g_all[...]).T)


def store_parts(refs, total, rows):
    middle, nearest, own = (total[j * rows : (j + 1) * rows, :].T for j in range(REACH - 1))
    refs[0][...], refs[2][...] = middle, own
    refs[1][:HD, :], refs[1][HD:, :] = encode(nearest)


def values_kernel(group, g_ref, w_ref, *refs):
    e_refs, dv_refs = refs[: REACH - 1], refs[REACH - 1 : 2 * (REACH - 1)]
    p_low, g_all = refs[2 * (REACH - 1) :]
    rows = g_ref.shape[0]
    per = rows // BLOCK
    blocks = REACH * per
    for g in range(group):
        g_all[g * rows : (g + 1) * rows, :] = g_ref[:, g * HD : (g + 1) * HD]
        for j in range(REACH - 1):
            for b in range(per):
                here = slice(b * BLOCK, (b + 1) * BLOCK)
                at = g * blocks + (j + 1) * per + b
                probs = e_refs[j][g, here, :] * w_ref[0, at : at + 1, :]
                there = slice(j * rows + b * BLOCK, j * rows + (b + 1) * BLOCK)
                p_low[there, g * rows : (g + 1) * rows] = probs.astype(jnp.bfloat16)
    dv = dot(p_low[...], g_all[...])
    store_parts(dv_refs, dv, rows)


def grads_kernel(group, rows, skip, q_ref, g_ref, gain_ref, w_ref, *refs):
    e_refs, k_refs, v_refs = (refs[i * REACH : (i + 1) * REACH] for i in range(3))
    refs = refs[3 * REACH + skip :]
    o_ref, dq_ref, gain_out, *dk_refs = refs[: REACH + 3]
    k_t, v_t, v_all, p_all, ds_all, q_all = refs[REACH + 3 :]
    per = rows // BLOCK
    blocks = REACH * per
    factor = 1.0 / math.sqrt(HD)
    for j in range(REACH):
        part = slice(j * rows, (j + 1) * rows)
        v_all[part, :] = v_refs[j][...]
        k_t[:, part] = k_refs[j][...].T
        v_t[:, part] = v_refs[j][...].T

    def probs_of(g, b):
        here = slice(b % per * BLOCK, (b % per + 1) * BLOCK)
        at = g * blocks + b
        return e_refs[b // per][g, here, :] * w_ref[0, at : at + 1, :]

    for g in range(group):
        cols = slice(g * HD, (g + 1) * HD)
        mine = slice(g * rows, (g + 1) * rows)
        q32 = q_ref[:, cols].astype(jnp.float32)
        gain = gain_ref[:, cols]
        q_all[mine, :] = (q32 * gain).astype(jnp.bfloat16)
        for b in range(blocks):
            p_all[g % 2, b * BLOCK : (b + 1) * BLOCK, :] = probs_of(g, b).astype(jnp.bfloat16)
        out_t = dot(v_t[...], p_all[g % 2]).astype(jnp.bfloat16)
        o_ref[:, cols] = out_t.T
        g_t = g_ref[:, cols].T
        delta = jnp.sum(g_t.astype(jnp.float32) * out_t.astype(jnp.float32), axis=0, keepdims=True)
        for b in range(blocks):
            here = slice(b * BLOCK, (b + 1) * BLOCK)
            ds = probs_of(g, b) * (dot(v_all[here, :], g_t) - delta)
            ds_all[here, mine] = ds.astype(jnp.bfloat16)
        dscaled = (dot(k_t[...], ds_all[:, mine]) * factor).T
        dq_ref[:, cols] = (dscaled * gain).astype(jnp.bfloat16)
        gain_out[:, cols] = jnp.sum(dscaled * q32, axis=0, keepdims=True)
    dk = dot(ds_all[...], q_all[...]) * factor
    dk_refs[0][:HD, :], dk_refs[0][HD:, :] = encode(dk[:rows, :].T)
    store_parts(dk_refs[1:], dk[rows:, :], rows)


def hop_kernel(kv_count, last, *refs):
    *messages, part, out = refs
    for c in range(kv_count):
        at, here = c * CODE_ROWS, slice(c * HD, (c + 1) * HD)
        total = part[here, :]
        for message in messages:
            total = total + decode(message[at : at + HD, :], message[at + HD : at + CODE_ROWS, :])
        if last:
            out[:, here] = total.T.astype(jnp.bfloat16)
        else:
            out[at : at + HD, :], out[at + HD : at + CODE_ROWS, :] = encode(total)


def hop(messages, part, last):
    kv_channels, rows = part.shape
    shape = jax.ShapeDtypeStruct((rows, kv_channels), jnp.bfloat16) if last else messages[0]
    return pl.pallas_call(
        functools.partial(hop_kernel, kv_channels // HD, last),
        out_shape=jax.ShapeDtypeStruct(shape.shape, shape.dtype),
        compiler_params=pltpu.CompilerParams(vmem_limit_bytes=8 * 2**20),
        cost_estimate=pl.CostEstimate(
            flops=10 * part.size, bytes_accessed=8 * part.size, transcendentals=0
        ),
        name="last_hop" if last else "hop",
    )(*messages, part)


class Shapes:
    def __init__(self, queries, keys, first=0):
        self.rows, self.channels = queries.shape
        self.kv_channels = keys.shape[1]
        self.kv_count = self.kv_channels // HD
        self.group = self.channels // self.kv_channels
        self.blocks = REACH * self.rows // BLOCK
        self.stat_rows = self.group * self.rows // BLOCK
        rows, group = self.rows, self.group
        self.wide = pl.BlockSpec((rows, group * HD), lambda c, *_: (0, c + first))
        self.line = pl.BlockSpec((1, group * HD), lambda c, *_: (0, c + first))
        self.thin = pl.BlockSpec((rows, HD), lambda c, *_: (0, c + first))
        self.code = pl.BlockSpec((CODE_ROWS, rows), lambda c, *_: (c + first, 0))
        self.part = pl.BlockSpec((HD, rows), lambda c, *_: (c + first, 0))
        self.heads = pl.BlockSpec((group, rows, rows), lambda c, *_: (c + first, 0, 0))
        self.stat = pl.BlockSpec((1, self.stat_rows, rows), lambda c, *_: (c + first, 0, 0))
        self.weight = pl.BlockSpec(
            (1, group * self.blocks, rows), lambda c, *_: (c + first, 0, 0)
        )

    def array(self, dtype, *shape):
        return jax.ShapeDtypeStruct(shape, dtype)

    def heads_array(self):
        return self.array(jnp.float32, self.kv_count * self.group, self.rows, self.rows)

    def stat_array(self):
        return self.array(jnp.float32, self.kv_count, self.stat_rows, self.rows)

    def weight_array(self):
        return self.array(jnp.float32, self.kv_count, self.group * self.blocks, self.rows)

    def code_array(self):
        return self.array(jnp.int16, self.kv_count * CODE_ROWS, self.rows)

    def part_array(self):
        return self.array(jnp.float32, self.kv_channels, self.rows)

    def cost(self, products, chunks, exps, count=None):
        heads = (self.kv_count if count is None else count) * self.group
        size = heads * chunks * self.rows * self.rows
        return pl.CostEstimate(
            flops=2 * products * size * HD, bytes_accessed=4 * size, transcendentals=exps * size
        )


def chunk_scores(queries, gain, keys, own):
    s = Shapes(queries, keys)
    return pl.pallas_call(
        functools.partial(scores_kernel, s.group, own),
        out_shape=[s.heads_array(), s.stat_array(), s.stat_array()],
        grid=(s.kv_count,),
        in_specs=[s.wide, s.line, s.thin],
        out_specs=[s.heads, s.stat, s.stat],
        compiler_params=pltpu.CompilerParams(vmem_limit_bytes=8 * 2**20),
        cost_estimate=s.cost(1, 1, 1),
        name="scores_own" if own else "scores",
    )(queries, gain, keys)


def far_scores(lo, queries, out_grad, gain, keys, stats):
    s = Shapes(queries, keys)
    return pl.pallas_call(
        functools.partial(far_kernel, s.group),
        out_shape=[s.heads_array(), s.weight_array(), s.code_array()],
        grid_spec=pltpu.PrefetchScalarGridSpec(
            num_scalar_prefetch=1,
            grid=(s.kv_count,),
            in_specs=[s.wide, s.wide, s.line, s.thin] + [s.stat] * len(stats),
            out_specs=[s.heads, s.weight, s.code],
            scratch_shapes=[
                pltpu.VMEM((s.rows, s.group * s.rows), jnp.bfloat16),
                pltpu.VMEM((s.group * s.rows, HD), jnp.bfloat16),
            ],
        ),
        compiler_params=pltpu.CompilerParams(vmem_limit_bytes=16 * 2**20),
        cost_estimate=s.cost(2, 1, 1),
        name="far_scores",
    )(lo, queries, out_grad, gain, keys, *stats)


def near_values(queries, keys, out_grad, weights, heads):
    s = Shapes(queries, keys)
    near = REACH - 1
    return pl.pallas_call(
        functools.partial(values_kernel, s.group),
        out_shape=[s.part_array(), s.code_array(), s.part_array()],
        grid=(s.kv_count,),
        in_specs=[s.wide, s.weight] + [s.heads] * near,
        out_specs=[s.part, s.code, s.part],
        scratch_shapes=[
            pltpu.VMEM((near * s.rows, s.group * s.rows), jnp.bfloat16),
            pltpu.VMEM((s.group * s.rows, HD), jnp.bfloat16),
        ],
        compiler_params=pltpu.CompilerParams(vmem_limit_bytes=15 * 2**20),
        cost_estimate=s.cost(1, near, 0),
        name="near_values",
    )(out_grad, weights, *heads)


def attention_grads(first, count, before, queries, out_grad, gain, weights, heads, keys, values):
    s = Shapes(queries, keys[0], first)
    width = REACH * s.rows
    n_in = 4 + 3 * REACH
    return pl.pallas_call(
        functools.partial(grads_kernel, s.group, s.rows, len(before)),
        out_shape=[s.array(jnp.bfloat16, s.rows, s.channels)] * 2
        + [s.array(jnp.float32, 1, s.channels)]
        + [s.code_array(), s.part_array()] * 2,
        grid=(count,),
        in_specs=[s.wide, s.wide, s.line, s.weight]
        + [s.heads] * REACH
        + [s.thin] * (2 * REACH)
        + [pl.BlockSpec(memory_space=pl.ANY)] * len(before),
        out_specs=[s.wide, s.wide, s.line] + [s.code, s.part] * 2,
        scratch_shapes=[
            pltpu.VMEM((HD, width), jnp.bfloat16),
            pltpu.VMEM((HD, width), jnp.bfloat16),
            pltpu.VMEM((width, HD), jnp.bfloat16),
            pltpu.VMEM((2, width, s.rows), jnp.bfloat16),
            pltpu.VMEM((width, s.group * s.rows), jnp.bfloat16),
            pltpu.VMEM((s.group * s.rows, HD), jnp.bfloat16),
        ],
        input_output_aliases={n_in + i: i for i in range(len(before))},
        compiler_params=pltpu.CompilerParams(vmem_limit_bytes=20 * 2**20),
        cost_estimate=s.cost(4, REACH, 0, count),
    )(queries, out_grad, gain, weights, *heads, *keys, *values, *before)


def step(queries, global_keys, global_values, out_grad, query_gain, doc_start):
    rows = queries.shape[1]
    device = lax.axis_index("ctx")
    q, do = queries[0], out_grad[0]
    gain = query_gain[None]
    together = lax.optimization_barrier
    lo = doc_start[0] * BLOCK - (device - (REACH - 1)) * rows
    lo, gain = together((lo, gain))
    own_keys, own_values = global_keys[0], global_values[0]
    near = [chunk_scores(q, gain, own_keys, True)]
    keys, values = [own_keys], [own_values]
    for i in range(1, REACH):
        keys.insert(0, shifted(keys[0], 1))
        if i < REACH - 1:
            near.insert(0, chunk_scores(q, gain, keys[0], False))
            values.insert(0, shifted(values[0], 1))
    values.insert(0, shifted(values[0], 1))
    half = own_keys.shape[1] // HD // 2

    stats = [stat for _, *pair in near for stat in pair]
    far, weights, moved = far_scores(lo, q, do, gain, keys[0], stats)
    heads = [far] + [e for e, *_ in near]
    dv_far = shifted(moved, -1)
    dv_middle, dv_near, dv_own = near_values(q, own_keys, do, weights, heads[1:])
    dv_near = shifted(dv_near, -1)
    early = attention_grads(0, half, [], q, do, gain, weights, heads, keys, values)
    dv_middle = shifted(hop([dv_far], dv_middle, False), -2)
    attn_out, query_grad, gain_term, dk_far, dk_middle, dk_near, dk_own = attention_grads(
        half, half, early, q, do, gain, weights, heads, keys, values
    )
    dk_far = shifted(dk_far, -1)
    dk_near = shifted(dk_near, -1)
    count = lax.axis_size("ctx")
    columns = [[i + z for i in range(0, count, Z_CHIPS)] for z in range(Z_CHIPS)]
    total = gathered_sum(gain_term, "dp", lax.axis_size("dp"))
    dk_far, total = together((dk_far, total))
    dk_middle = shifted(hop([dk_far], dk_middle, False), -2)
    total = gathered_sum(total, "ctx", count // Z_CHIPS, columns)
    total = pair_sum(total, 1)
    total = pair_sum(total, 2)
    gain_grad = pair_sum(total, 4)
    value_grad = hop([dv_middle, dv_near], dv_own, True)
    key_grad = hop([dk_middle, dk_near], dk_own, True)
    return (
        attn_out[None],
        query_grad[None],
        key_grad[None],
        value_grad[None],
        gain_grad[0],
    )


def solution(mesh):
    rows = P("dp", "ctx", None)
    return jax.shard_map(
        step,
        mesh=mesh,
        in_specs=(rows, rows, rows, rows, P(), P("dp", "ctx")),
        out_specs=(rows, rows, rows, rows, P()),
        check_vma=False,
    )
```

```python
import functools
import math

import jax
import jax.numpy as jnp
from jax import lax
from jax.experimental import pallas as pl
from jax.experimental.pallas import tpu as pltpu
from jax.sharding import PartitionSpec as P


HD = 128
BLOCK = 128
REACH = 4
Z_CHIPS = 8
EXPONENT = 1.4426950408889634 / math.sqrt(HD)
SCALE_STEPS = 64.0
SCALE_ROWS = 16
CODE_MAX = 32767.0
CODE_ROWS = HD + SCALE_ROWS


def shifted(value, steps):
    count = lax.axis_size("ctx")
    first, last = (max(0, -steps), min(count, count - steps))
    pairs = [(source, source + steps) for source in range(first, last)]
    return lax.ppermute(value, "ctx", pairs)


def gathered_sum(value, axis, size, groups=None):
    copies = jnp.broadcast_to(value[None], (size, *value.shape))
    parts = lax.all_to_all(copies, axis, 0, 0, tiled=True, axis_index_groups=groups)
    return jnp.sum(parts, axis=0)


def ring_kernel(place, parts, out):
    count = parts.shape[0]
    total = parts[pl.ds(place[0], 1), :]
    for r in range(1, count):
        total = total + parts[pl.ds((place[0] + r) % count, 1), :]
    out[...] = total


def ring_sum(value):
    count = lax.axis_size("ctx")
    step = 1
    while step < Z_CHIPS:
        pairs = [
            (i, i - i % Z_CHIPS + (i + step) % Z_CHIPS) for i in range(count)
        ]
        value = jnp.concatenate([value, lax.ppermute(value, "ctx", pairs)], axis=0)
        step *= 2
    place = (lax.axis_index("ctx") % Z_CHIPS).reshape(1)
    return pl.pallas_call(
        ring_kernel,
        out_shape=jax.ShapeDtypeStruct((1, value.shape[1]), jnp.float32),
        in_specs=[
            pl.BlockSpec(memory_space=pltpu.SMEM),
            pl.BlockSpec(memory_space=pltpu.VMEM),
        ],
        out_specs=pl.BlockSpec(memory_space=pltpu.VMEM),
        compiler_params=pltpu.CompilerParams(vmem_limit_bytes=4 * 2**20),
        name="ring_sum",
    )(place, value)


def encode(value):
    top = jnp.maximum(jnp.max(jnp.abs(value), axis=0, keepdims=True), 2.0**-100)
    level = jnp.ceil(jnp.log2(top) * SCALE_STEPS)
    coded = jnp.round(value * (jnp.exp2(level * (-1.0 / SCALE_STEPS)) * CODE_MAX))
    level = jnp.broadcast_to(level, (SCALE_ROWS, value.shape[1]))
    return tuple(v.astype(jnp.int32).astype(jnp.int16) for v in (coded, level))


def decode(coded, level):
    level = level.astype(jnp.int32).astype(jnp.float32)[:1]
    return coded.astype(jnp.int32).astype(jnp.float32) * (
        jnp.exp2(level * (1.0 / SCALE_STEPS)) * (1.0 / CODE_MAX)
    )


def dot(a, b, dims=((1,), (0,))):
    return lax.dot_general(a, b, (dims, ((), ())), preferred_element_type=jnp.float32)


def softened(raw):
    top = jnp.max(raw, axis=0, keepdims=True)
    e = jnp.exp2((raw - top) * EXPONENT)
    return e, top, jnp.sum(e, axis=0, keepdims=True)


def scaled_query(q_ref, gain_ref, cols):
    return (q_ref[:, cols].astype(jnp.float32) * gain_ref[:, cols]).astype(jnp.bfloat16)


def scores_kernel(group, own, q_ref, gain_ref, k_ref, e_ref, top_ref, sum_ref):
    rows = k_ref.shape[0]
    per = rows // BLOCK
    if own:
        key = lax.broadcasted_iota(jnp.int32, (BLOCK, rows), 0)
        query = lax.broadcasted_iota(jnp.int32, (BLOCK, rows), 1)
    for g in range(group):
        scaled = scaled_query(q_ref, gain_ref, slice(g * HD, (g + 1) * HD))
        for b in range(per):
            here = slice(b * BLOCK, (b + 1) * BLOCK)
            raw = dot(k_ref[here, :], scaled, ((1,), (1,)))
            if own:
                later = (key + b * BLOCK > query) & (query >= b * BLOCK)
                raw = jnp.where(later, -jnp.inf, raw)
            e, top, total = softened(raw)
            at = slice(g * per + b, g * per + b + 1)
            e_ref[g, here, :], top_ref[0, at, :], sum_ref[0, at, :] = e, top, total


def far_kernel(group, lo, q_ref, g_ref, gain_ref, k_ref, *refs):
    stats = refs[: 2 * (REACH - 1)]
    e_ref, w_ref, dv_ref, p_low, g_all = refs[2 * (REACH - 1) :]
    rows = k_ref.shape[0]
    per = rows // BLOCK
    blocks = REACH * per
    half = lax.broadcasted_iota(jnp.int32, (1, rows), 1) // BLOCK
    begin = jnp.where(half == 0, lo[0], lo[1])
    allowed = [
        (begin <= b * BLOCK) & (half >= b - (REACH - 1) * per) for b in range(blocks)
    ]
    for g in range(group):
        cols = slice(g * HD, (g + 1) * HD)
        g_all[g * rows : (g + 1) * rows, :] = g_ref[:, cols]
        scaled = scaled_query(q_ref, gain_ref, cols)
        tops, sums = [], []
        for b in range(per):
            here = slice(b * BLOCK, (b + 1) * BLOCK)
            e, top, total = softened(dot(k_ref[here, :], scaled, ((1,), (1,))))
            e_ref[g, here, :] = e
            tops.append(top)
            sums.append(total)
        for j in range(REACH - 1):
            for b in range(per):
                at = slice(g * per + b, g * per + b + 1)
                tops.append(stats[2 * j][0, at, :])
                sums.append(stats[2 * j + 1][0, at, :])
        tops = [jnp.where(ok, top, -jnp.inf) for ok, top in zip(allowed, tops, strict=True)]
        highest = functools.reduce(jnp.maximum, tops)
        shares = [jnp.exp2((top - highest) * EXPONENT) for top in tops]
        total = sum(share * part for share, part in zip(shares, sums, strict=True))
        inverse = 1.0 / total
        for b in range(blocks):
            weight = shares[b] * inverse
            w_ref[0, g * blocks + b : g * blocks + b + 1, :] = weight
            if b < per:
                here = slice(b * BLOCK, (b + 1) * BLOCK)
                p_low[here, g * rows : (g + 1) * rows] = (e_ref[g, here, :] * weight).astype(
                    jnp.bfloat16
                )
    dv_ref[0, :HD, :], dv_ref[0, HD:, :] = encode(dot(p_low[...], g_all[...]).T)


def store_parts(middle_ref, near_ref, own_ref, total, rows):
    middle, nearest, own = (total[j * rows : (j + 1) * rows, :].T for j in range(REACH - 1))
    middle_ref[...], own_ref[...] = middle, own
    near_ref[:HD, :], near_ref[HD:, :] = encode(nearest)


def values_kernel(group, g_ref, w_ref, *refs):
    e_refs, dv_refs = refs[: REACH - 1], refs[REACH - 1 : 2 * (REACH - 1)]
    p_low, g_all = refs[2 * (REACH - 1) :]
    rows = g_ref.shape[0]
    per = rows // BLOCK
    blocks = REACH * per
    for g in range(group):
        g_all[g * rows : (g + 1) * rows, :] = g_ref[:, g * HD : (g + 1) * HD]
        for j in range(REACH - 1):
            for b in range(per):
                here = slice(b * BLOCK, (b + 1) * BLOCK)
                at = g * blocks + (j + 1) * per + b
                probs = e_refs[j][g, here, :] * w_ref[0, at : at + 1, :]
                there = slice(j * rows + b * BLOCK, j * rows + (b + 1) * BLOCK)
                p_low[there, g * rows : (g + 1) * rows] = probs.astype(jnp.bfloat16)
    dv = dot(p_low[...], g_all[...])
    store_parts(dv_refs[0], dv_refs[1].at[0], dv_refs[2], dv, rows)


def grads_kernel(group, rows, skip, q_ref, g_ref, gain_ref, w_ref, *refs):
    e_refs, k_refs, v_refs = (refs[i * REACH : (i + 1) * REACH] for i in range(3))
    refs = refs[3 * REACH + skip :]
    o_ref, dq_ref, gain_out, *dk_refs = refs[:6]
    k_t, v_t, v_all, p_all, ds_all, q_all = refs[6:]
    per = rows // BLOCK
    blocks = REACH * per
    factor = 1.0 / math.sqrt(HD)
    for j in range(REACH):
        part = slice(j * rows, (j + 1) * rows)
        v_all[part, :] = v_refs[j][...]
        k_t[:, part] = k_refs[j][...].T
        v_t[:, part] = v_refs[j][...].T

    def probs_of(g, b):
        here = slice(b % per * BLOCK, (b % per + 1) * BLOCK)
        at = g * blocks + b
        return e_refs[b // per][g, here, :] * w_ref[0, at : at + 1, :]

    for g in range(group):
        cols = slice(g * HD, (g + 1) * HD)
        mine = slice(g * rows, (g + 1) * rows)
        q32 = q_ref[:, cols].astype(jnp.float32)
        gain = gain_ref[:, cols]
        q_all[mine, :] = (q32 * gain).astype(jnp.bfloat16)
        for b in range(blocks):
            p_all[g % 2, b * BLOCK : (b + 1) * BLOCK, :] = probs_of(g, b).astype(jnp.bfloat16)
        out_t = dot(v_t[...], p_all[g % 2]).astype(jnp.bfloat16)
        o_ref[:, cols] = out_t.T
        g_t = g_ref[:, cols].T
        delta = jnp.sum(g_t.astype(jnp.float32) * out_t.astype(jnp.float32), axis=0, keepdims=True)
        for b in range(blocks):
            here = slice(b * BLOCK, (b + 1) * BLOCK)
            ds = probs_of(g, b) * (dot(v_all[here, :], g_t) - delta)
            ds_all[here, mine] = ds.astype(jnp.bfloat16)
        dscaled = (dot(k_t[...], ds_all[:, mine]) * factor).T
        dq_ref[:, cols] = (dscaled * gain).astype(jnp.bfloat16)
        gain_out[:, cols] = jnp.sum(dscaled * q32, axis=0, keepdims=True)
    dk = dot(ds_all[...], q_all[...]) * factor
    dk_codes, dk_middle, dk_own = dk_refs
    dk_codes[0, :HD, :], dk_codes[0, HD:, :] = encode(dk[:rows, :].T)
    store_parts(dk_middle, dk_codes.at[1], dk_own, dk[rows:, :], rows)


def hop_kernel(kv_count, picks, last, *refs):
    *messages, part, out = refs
    for c in range(kv_count):
        at, here = c * CODE_ROWS, slice(c * HD, (c + 1) * HD)
        total = part[here, :]
        for message, pick in zip(messages, picks, strict=True):
            total = total + decode(
                message[pick, at : at + HD, :], message[pick, at + HD : at + CODE_ROWS, :]
            )
        if last:
            out[:, here] = total.T.astype(jnp.bfloat16)
        else:
            out[0, at : at + HD, :], out[0, at + HD : at + CODE_ROWS, :] = encode(total)


def hop(messages, part, last):
    kv_channels, rows = part.shape
    messages, picks = zip(*messages, strict=True)
    shape = (
        jax.ShapeDtypeStruct((rows, kv_channels), jnp.bfloat16)
        if last
        else jax.ShapeDtypeStruct((1, *messages[0].shape[1:]), jnp.int16)
    )
    return pl.pallas_call(
        functools.partial(hop_kernel, kv_channels // HD, picks, last),
        out_shape=jax.ShapeDtypeStruct(shape.shape, shape.dtype),
        compiler_params=pltpu.CompilerParams(vmem_limit_bytes=8 * 2**20),
        cost_estimate=pl.CostEstimate(
            flops=10 * part.size, bytes_accessed=8 * part.size, transcendentals=0
        ),
        name="last_hop" if last else "hop",
    )(*messages, part)


class Shapes:
    def __init__(self, queries, keys, first=0):
        self.rows, self.channels = queries.shape
        self.kv_channels = keys.shape[1]
        self.kv_count = self.kv_channels // HD
        self.group = self.channels // self.kv_channels
        self.blocks = REACH * self.rows // BLOCK
        self.stat_rows = self.group * self.rows // BLOCK
        rows, group = self.rows, self.group
        self.wide = pl.BlockSpec((rows, group * HD), lambda c, *_: (0, c + first))
        self.line = pl.BlockSpec((1, group * HD), lambda c, *_: (0, c + first))
        self.thin = pl.BlockSpec((rows, HD), lambda c, *_: (0, c + first))
        self.code, self.codes = (
            pl.BlockSpec((n, CODE_ROWS, rows), lambda c, *_: (0, c + first, 0)) for n in (1, 2)
        )
        self.part = pl.BlockSpec((HD, rows), lambda c, *_: (c + first, 0))
        self.heads = pl.BlockSpec((group, rows, rows), lambda c, *_: (c + first, 0, 0))
        self.stat = pl.BlockSpec((1, self.stat_rows, rows), lambda c, *_: (c + first, 0, 0))
        self.weight = pl.BlockSpec(
            (1, group * self.blocks, rows), lambda c, *_: (c + first, 0, 0)
        )

    def array(self, dtype, *shape):
        return jax.ShapeDtypeStruct(shape, dtype)

    def heads_array(self):
        return self.array(jnp.float32, self.kv_count * self.group, self.rows, self.rows)

    def stat_array(self):
        return self.array(jnp.float32, self.kv_count, self.stat_rows, self.rows)

    def weight_array(self):
        return self.array(jnp.float32, self.kv_count, self.group * self.blocks, self.rows)

    def code_array(self, count=1):
        return self.array(jnp.int16, count, self.kv_count * CODE_ROWS, self.rows)

    def part_array(self):
        return self.array(jnp.float32, self.kv_channels, self.rows)

    def cost(self, products, chunks, exps, count=None):
        heads = (self.kv_count if count is None else count) * self.group
        size = heads * chunks * self.rows * self.rows
        return pl.CostEstimate(
            flops=2 * products * size * HD, bytes_accessed=4 * size, transcendentals=exps * size
        )


def chunk_scores(queries, gain, keys, own):
    s = Shapes(queries, keys)
    return pl.pallas_call(
        functools.partial(scores_kernel, s.group, own),
        out_shape=[s.heads_array(), s.stat_array(), s.stat_array()],
        grid=(s.kv_count,),
        in_specs=[s.wide, s.line, s.thin],
        out_specs=[s.heads, s.stat, s.stat],
        compiler_params=pltpu.CompilerParams(vmem_limit_bytes=8 * 2**20),
        cost_estimate=s.cost(1, 1, 1),
        name="scores_own" if own else "scores",
    )(queries, gain, keys)


def far_scores(lo, queries, out_grad, gain, keys, stats):
    s = Shapes(queries, keys)
    return pl.pallas_call(
        functools.partial(far_kernel, s.group),
        out_shape=[s.heads_array(), s.weight_array(), s.code_array()],
        grid_spec=pltpu.PrefetchScalarGridSpec(
            num_scalar_prefetch=1,
            grid=(s.kv_count,),
            in_specs=[s.wide, s.wide, s.line, s.thin] + [s.stat] * len(stats),
            out_specs=[s.heads, s.weight, s.code],
            scratch_shapes=[
                pltpu.VMEM((s.rows, s.group * s.rows), jnp.bfloat16),
                pltpu.VMEM((s.group * s.rows, HD), jnp.bfloat16),
            ],
        ),
        compiler_params=pltpu.CompilerParams(vmem_limit_bytes=16 * 2**20),
        cost_estimate=s.cost(2, 1, 1),
        name="far_scores",
    )(lo, queries, out_grad, gain, keys, *stats)


def near_values(queries, keys, out_grad, weights, heads):
    s = Shapes(queries, keys)
    near = REACH - 1
    return pl.pallas_call(
        functools.partial(values_kernel, s.group),
        out_shape=[s.part_array(), s.code_array(), s.part_array()],
        grid=(s.kv_count,),
        in_specs=[s.wide, s.weight] + [s.heads] * near,
        out_specs=[s.part, s.code, s.part],
        scratch_shapes=[
            pltpu.VMEM((near * s.rows, s.group * s.rows), jnp.bfloat16),
            pltpu.VMEM((s.group * s.rows, HD), jnp.bfloat16),
        ],
        compiler_params=pltpu.CompilerParams(vmem_limit_bytes=15 * 2**20),
        cost_estimate=s.cost(1, near, 0),
        name="near_values",
    )(out_grad, weights, *heads)


def attention_grads(first, count, before, queries, out_grad, gain, weights, heads, keys, values):
    s = Shapes(queries, keys[0], first)
    width = REACH * s.rows
    n_in = 4 + 3 * REACH
    return pl.pallas_call(
        functools.partial(grads_kernel, s.group, s.rows, len(before)),
        out_shape=[s.array(jnp.bfloat16, s.rows, s.channels)] * 2
        + [s.array(jnp.float32, 1, s.channels)]
        + [s.code_array(2), s.part_array(), s.part_array()],
        grid=(count,),
        in_specs=[s.wide, s.wide, s.line, s.weight]
        + [s.heads] * REACH
        + [s.thin] * (2 * REACH)
        + [pl.BlockSpec(memory_space=pl.ANY)] * len(before),
        out_specs=[s.wide, s.wide, s.line, s.codes, s.part, s.part],
        scratch_shapes=[
            pltpu.VMEM((HD, width), jnp.bfloat16),
            pltpu.VMEM((HD, width), jnp.bfloat16),
            pltpu.VMEM((width, HD), jnp.bfloat16),
            pltpu.VMEM((2, width, s.rows), jnp.bfloat16),
            pltpu.VMEM((width, s.group * s.rows), jnp.bfloat16),
            pltpu.VMEM((s.group * s.rows, HD), jnp.bfloat16),
        ],
        input_output_aliases={n_in + i: i for i in range(len(before))},
        compiler_params=pltpu.CompilerParams(vmem_limit_bytes=20 * 2**20),
        cost_estimate=s.cost(4, REACH, 0, count),
    )(queries, out_grad, gain, weights, *heads, *keys, *values, *before)


def step(queries, global_keys, global_values, out_grad, query_gain, doc_start):
    rows = queries.shape[1]
    device = lax.axis_index("ctx")
    q, do = queries[0], out_grad[0]
    gain = query_gain[None]
    together = lax.optimization_barrier
    lo = doc_start[0] * BLOCK - (device - (REACH - 1)) * rows
    lo, gain = together((lo, gain))
    own_keys, own_values = global_keys[0], global_values[0]
    near = [chunk_scores(q, gain, own_keys, True)]
    keys, values = [own_keys], [own_values]
    for i in range(1, REACH):
        keys.insert(0, shifted(keys[0], 1))
        if i < REACH - 1:
            near.insert(0, chunk_scores(q, gain, keys[0], False))
            values.insert(0, shifted(values[0], 1))
    values.insert(0, shifted(values[0], 1))
    half = own_keys.shape[1] // HD // 2

    stats = [stat for _, *pair in near for stat in pair]
    far, weights, moved = far_scores(lo, q, do, gain, keys[0], stats)
    heads = [far] + [e for e, *_ in near]
    dv_far = shifted(moved, -1)
    dv_middle, dv_near, dv_own = near_values(q, own_keys, do, weights, heads[1:])
    dv_near = shifted(dv_near, -1)
    early = attention_grads(0, half, [], q, do, gain, weights, heads, keys, values)
    dv_middle = shifted(hop([(dv_far, 0)], dv_middle, False), -2)
    attn_out, query_grad, gain_term, dk_codes, dk_middle, dk_own = attention_grads(
        half, half, early, q, do, gain, weights, heads, keys, values
    )
    dk_codes = shifted(dk_codes, -1)
    count = lax.axis_size("ctx")
    columns = [[i + z for i in range(0, count, Z_CHIPS)] for z in range(Z_CHIPS)]
    total = gathered_sum(gain_term, "dp", lax.axis_size("dp"))
    total = gathered_sum(total, "ctx", count // Z_CHIPS, columns)
    dk_codes, total = together((dk_codes, total))
    dk_middle = shifted(hop([(dk_codes, 0)], dk_middle, False), -2)
    gain_grad = ring_sum(total)
    value_grad = hop([(dv_middle, 0), (dv_near, 0)], dv_own, True)
    key_grad = hop([(dk_middle, 0), (dk_codes, 1)], dk_own, True)
    return (
        attn_out[None],
        query_grad[None],
        key_grad[None],
        value_grad[None],
        gain_grad[0],
    )


def solution(mesh):
    rows = P("dp", "ctx", None)
    return jax.shard_map(
        step,
        mesh=mesh,
        in_specs=(rows, rows, rows, rows, P(), P("dp", "ctx")),
        out_specs=(rows, rows, rows, rows, P()),
        check_vma=False,
    )
```

```python
import functools
import math

import jax
import jax.numpy as jnp
from jax import lax
from jax.experimental import pallas as pl
from jax.experimental.pallas import tpu as pltpu
from jax.sharding import PartitionSpec as P


HD = 128
BLOCK = 128
REACH = 4
Z_CHIPS = 8
EXPONENT = 1.4426950408889634 / math.sqrt(HD)
SCALE_STEPS = 64.0
SCALE_ROWS = 16
CODE_MAX = 32767.0
CODE_ROWS = HD + SCALE_ROWS


def shifted(value, steps):
    count = lax.axis_size("ctx")
    first, last = (max(0, -steps), min(count, count - steps))
    pairs = [(source, source + steps) for source in range(first, last)]
    return lax.ppermute(value, "ctx", pairs)


def gathered_sum(value, axis, size, groups=None):
    copies = jnp.broadcast_to(value[None], (size, *value.shape))
    parts = lax.all_to_all(copies, axis, 0, 0, tiled=True, axis_index_groups=groups)
    return jnp.sum(parts, axis=0)


def ring_kernel(place, parts, out):
    count = parts.shape[0]
    total = parts[pl.ds(place[0], 1), :]
    for r in range(1, count):
        total = total + parts[pl.ds((place[0] + r) % count, 1), :]
    out[...] = total


def ring_sum(value):
    count = lax.axis_size("ctx")
    step = 1
    while step < Z_CHIPS:
        pairs = [
            (i, i - i % Z_CHIPS + (i + step) % Z_CHIPS) for i in range(count)
        ]
        value = jnp.concatenate([value, lax.ppermute(value, "ctx", pairs)], axis=0)
        step *= 2
    place = (lax.axis_index("ctx") % Z_CHIPS).reshape(1)
    return pl.pallas_call(
        ring_kernel,
        out_shape=jax.ShapeDtypeStruct((1, value.shape[1]), jnp.float32),
        in_specs=[
            pl.BlockSpec(memory_space=pltpu.SMEM),
            pl.BlockSpec(memory_space=pltpu.VMEM),
        ],
        out_specs=pl.BlockSpec(memory_space=pltpu.VMEM),
        compiler_params=pltpu.CompilerParams(vmem_limit_bytes=4 * 2**20),
        name="ring_sum",
    )(place, value)


def encode(value):
    top = jnp.maximum(jnp.max(jnp.abs(value), axis=0, keepdims=True), 2.0**-100)
    level = jnp.ceil(jnp.log2(top) * SCALE_STEPS)
    coded = jnp.round(value * (jnp.exp2(level * (-1.0 / SCALE_STEPS)) * CODE_MAX))
    level = jnp.broadcast_to(level, (SCALE_ROWS, value.shape[1]))
    return tuple(v.astype(jnp.int32).astype(jnp.int16) for v in (coded, level))


def decode(coded, level):
    level = level.astype(jnp.int32).astype(jnp.float32)[:1]
    return coded.astype(jnp.int32).astype(jnp.float32) * (
        jnp.exp2(level * (1.0 / SCALE_STEPS)) * (1.0 / CODE_MAX)
    )


def dot(a, b, dims=((1,), (0,))):
    return lax.dot_general(a, b, (dims, ((), ())), preferred_element_type=jnp.float32)


def softened(raw):
    top = jnp.max(raw, axis=0, keepdims=True)
    e = jnp.exp2((raw - top) * EXPONENT)
    return e, top, jnp.sum(e, axis=0, keepdims=True)


def scaled_query(q_ref, gain_ref, cols):
    return (q_ref[:, cols].astype(jnp.float32) * gain_ref[:, cols]).astype(jnp.bfloat16)


def scores_kernel(group, own, q_ref, gain_ref, k_ref, e_ref, top_ref, sum_ref):
    rows = k_ref.shape[0]
    per = rows // BLOCK
    if own:
        key = lax.broadcasted_iota(jnp.int32, (BLOCK, rows), 0)
        query = lax.broadcasted_iota(jnp.int32, (BLOCK, rows), 1)
    for g in range(group):
        scaled = scaled_query(q_ref, gain_ref, slice(g * HD, (g + 1) * HD))
        for b in range(per):
            here = slice(b * BLOCK, (b + 1) * BLOCK)
            raw = dot(k_ref[here, :], scaled, ((1,), (1,)))
            if own:
                later = (key + b * BLOCK > query) & (query >= b * BLOCK)
                raw = jnp.where(later, -jnp.inf, raw)
            e, top, total = softened(raw)
            at = slice(g * per + b, g * per + b + 1)
            e_ref[g, here, :], top_ref[0, at, :], sum_ref[0, at, :] = e, top, total


def far_kernel(group, lo, q_ref, g_ref, gain_ref, k_ref, *refs):
    stats = refs[: 2 * (REACH - 1)]
    near_ref, e_ref, w_ref, dv_ref, p_low, g_all = refs[2 * (REACH - 1) :]
    rows = k_ref.shape[0]
    per = rows // BLOCK
    blocks = REACH * per
    half = lax.broadcasted_iota(jnp.int32, (1, rows), 1) // BLOCK
    begin = jnp.where(half == 0, lo[0], lo[1])
    allowed = [
        (begin <= b * BLOCK) & (half >= b - (REACH - 1) * per) for b in range(blocks)
    ]
    for g in range(group):
        cols = slice(g * HD, (g + 1) * HD)
        g_all[g * rows : (g + 1) * rows, :] = g_ref[:, cols]
        scaled = scaled_query(q_ref, gain_ref, cols)
        tops, sums = [], []
        for b in range(per):
            here = slice(b * BLOCK, (b + 1) * BLOCK)
            e, top, total = softened(dot(k_ref[here, :], scaled, ((1,), (1,))))
            e_ref[g, here, :] = e
            tops.append(top)
            sums.append(total)
        for j in range(REACH - 1):
            for b in range(per):
                at = slice(g * per + b, g * per + b + 1)
                tops.append(stats[2 * j][0, at, :])
                sums.append(stats[2 * j + 1][0, at, :])
        tops = [jnp.where(ok, top, -jnp.inf) for ok, top in zip(allowed, tops, strict=True)]
        highest = functools.reduce(jnp.maximum, tops)
        shares = [jnp.exp2((top - highest) * EXPONENT) for top in tops]
        total = sum(share * part for share, part in zip(shares, sums, strict=True))
        inverse = 1.0 / total
        for b in range(blocks):
            weight = shares[b] * inverse
            w_ref[0, g * blocks + b : g * blocks + b + 1, :] = weight
            chunk, b = b // per, b % per
            if chunk in (0, REACH - 2):
                here = slice(b * BLOCK, (b + 1) * BLOCK)
                e = (near_ref if chunk else e_ref)[g, here, :]
                at = (rows if chunk else 0) + b * BLOCK
                p_low[at : at + BLOCK, g * rows : (g + 1) * rows] = (e * weight).astype(
                    jnp.bfloat16
                )
    dv = dot(p_low[...], g_all[...])
    for i in range(2):
        part = dv[i * rows : (i + 1) * rows, :].T
        dv_ref[i, :HD, :], dv_ref[i, HD:, :] = encode(part)


def values_kernel(group, g_ref, w_ref, *refs):
    e_refs, dv_refs, (p_low, g_all) = refs[:2], refs[2:4], refs[4:]
    rows = g_ref.shape[0]
    per = rows // BLOCK
    blocks = REACH * per
    for g in range(group):
        g_all[g * rows : (g + 1) * rows, :] = g_ref[:, g * HD : (g + 1) * HD]
        for j, chunk in enumerate((1, REACH - 1)):
            for b in range(per):
                here = slice(b * BLOCK, (b + 1) * BLOCK)
                at = g * blocks + chunk * per + b
                probs = e_refs[j][g, here, :] * w_ref[0, at : at + 1, :]
                there = slice(j * rows + b * BLOCK, j * rows + (b + 1) * BLOCK)
                p_low[there, g * rows : (g + 1) * rows] = probs.astype(jnp.bfloat16)
    dv = dot(p_low[...], g_all[...])
    for j in range(2):
        dv_refs[j][...] = dv[j * rows : (j + 1) * rows, :].T


def grads_kernel(group, rows, skip, q_ref, g_ref, gain_ref, w_ref, *refs):
    e_refs, k_refs, v_refs = (refs[i * REACH : (i + 1) * REACH] for i in range(3))
    refs = refs[3 * REACH + skip :]
    o_ref, dq_ref, gain_out, *dk_refs = refs[:6]
    k_t, v_t, v_all, p_all, ds_all, q_all = refs[6:]
    per = rows // BLOCK
    blocks = REACH * per
    factor = 1.0 / math.sqrt(HD)
    for j in range(REACH):
        part = slice(j * rows, (j + 1) * rows)
        v_all[part, :] = v_refs[j][...]
        k_t[:, part] = k_refs[j][...].T
        v_t[:, part] = v_refs[j][...].T

    def probs_of(g, b):
        here = slice(b % per * BLOCK, (b % per + 1) * BLOCK)
        at = g * blocks + b
        return e_refs[b // per][g, here, :] * w_ref[0, at : at + 1, :]

    for g in range(group):
        cols = slice(g * HD, (g + 1) * HD)
        mine = slice(g * rows, (g + 1) * rows)
        q32 = q_ref[:, cols].astype(jnp.float32)
        gain = gain_ref[:, cols]
        q_all[mine, :] = (q32 * gain).astype(jnp.bfloat16)
        for b in range(blocks):
            p_all[g % 2, b * BLOCK : (b + 1) * BLOCK, :] = probs_of(g, b).astype(jnp.bfloat16)
        out_t = dot(v_t[...], p_all[g % 2]).astype(jnp.bfloat16)
        o_ref[:, cols] = out_t.T
        g_t = g_ref[:, cols].T
        delta = jnp.sum(g_t.astype(jnp.float32) * out_t.astype(jnp.float32), axis=0, keepdims=True)
        for b in range(blocks):
            here = slice(b * BLOCK, (b + 1) * BLOCK)
            ds = probs_of(g, b) * (dot(v_all[here, :], g_t) - delta)
            ds_all[here, mine] = ds.astype(jnp.bfloat16)
        dscaled = (dot(k_t[...], ds_all[:, mine]) * factor).T
        dq_ref[:, cols] = (dscaled * gain).astype(jnp.bfloat16)
        gain_out[:, cols] = jnp.sum(dscaled * q32, axis=0, keepdims=True)
    dk = dot(ds_all[...], q_all[...]) * factor
    dk_codes, dk_middle, dk_own = dk_refs
    far, middle, nearest, own = (dk[j * rows : (j + 1) * rows, :].T for j in range(REACH))
    dk_middle[...], dk_own[...] = middle, own
    for i, part in enumerate((far, nearest)):
        dk_codes[i, :HD, :], dk_codes[i, HD:, :] = encode(part)


def hop_kernel(kv_count, picks, last, *refs):
    *messages, part, out = refs
    for c in range(kv_count):
        at, here = c * CODE_ROWS, slice(c * HD, (c + 1) * HD)
        total = part[here, :]
        for message, pick in zip(messages, picks, strict=True):
            total = total + decode(
                message[pick, at : at + HD, :], message[pick, at + HD : at + CODE_ROWS, :]
            )
        if last:
            out[:, here] = total.T.astype(jnp.bfloat16)
        else:
            out[0, at : at + HD, :], out[0, at + HD : at + CODE_ROWS, :] = encode(total)


def hop(messages, part, last):
    kv_channels, rows = part.shape
    messages, picks = zip(*messages, strict=True)
    shape = (
        jax.ShapeDtypeStruct((rows, kv_channels), jnp.bfloat16)
        if last
        else jax.ShapeDtypeStruct((1, *messages[0].shape[1:]), jnp.int16)
    )
    return pl.pallas_call(
        functools.partial(hop_kernel, kv_channels // HD, picks, last),
        out_shape=jax.ShapeDtypeStruct(shape.shape, shape.dtype),
        compiler_params=pltpu.CompilerParams(vmem_limit_bytes=8 * 2**20),
        cost_estimate=pl.CostEstimate(
            flops=10 * part.size, bytes_accessed=8 * part.size, transcendentals=0
        ),
        name="last_hop" if last else "hop",
    )(*messages, part)


class Shapes:
    def __init__(self, queries, keys, first=0):
        self.rows, self.channels = queries.shape
        self.kv_channels = keys.shape[1]
        self.kv_count = self.kv_channels // HD
        self.group = self.channels // self.kv_channels
        self.blocks = REACH * self.rows // BLOCK
        self.stat_rows = self.group * self.rows // BLOCK
        rows, group = self.rows, self.group
        self.wide = pl.BlockSpec((rows, group * HD), lambda c, *_: (0, c + first))
        self.line = pl.BlockSpec((1, group * HD), lambda c, *_: (0, c + first))
        self.thin = pl.BlockSpec((rows, HD), lambda c, *_: (0, c + first))
        self.code, self.codes = (
            pl.BlockSpec((n, CODE_ROWS, rows), lambda c, *_: (0, c + first, 0)) for n in (1, 2)
        )
        self.part = pl.BlockSpec((HD, rows), lambda c, *_: (c + first, 0))
        self.heads = pl.BlockSpec((group, rows, rows), lambda c, *_: (c + first, 0, 0))
        self.stat = pl.BlockSpec((1, self.stat_rows, rows), lambda c, *_: (c + first, 0, 0))
        self.weight = pl.BlockSpec(
            (1, group * self.blocks, rows), lambda c, *_: (c + first, 0, 0)
        )

    def array(self, dtype, *shape):
        return jax.ShapeDtypeStruct(shape, dtype)

    def heads_array(self):
        return self.array(jnp.float32, self.kv_count * self.group, self.rows, self.rows)

    def stat_array(self):
        return self.array(jnp.float32, self.kv_count, self.stat_rows, self.rows)

    def weight_array(self):
        return self.array(jnp.float32, self.kv_count, self.group * self.blocks, self.rows)

    def code_array(self, count=1):
        return self.array(jnp.int16, count, self.kv_count * CODE_ROWS, self.rows)

    def part_array(self):
        return self.array(jnp.float32, self.kv_channels, self.rows)

    def cost(self, products, chunks, exps, count=None):
        heads = (self.kv_count if count is None else count) * self.group
        size = heads * chunks * self.rows * self.rows
        return pl.CostEstimate(
            flops=2 * products * size * HD, bytes_accessed=4 * size, transcendentals=exps * size
        )


def chunk_scores(queries, gain, keys, own):
    s = Shapes(queries, keys)
    return pl.pallas_call(
        functools.partial(scores_kernel, s.group, own),
        out_shape=[s.heads_array(), s.stat_array(), s.stat_array()],
        grid=(s.kv_count,),
        in_specs=[s.wide, s.line, s.thin],
        out_specs=[s.heads, s.stat, s.stat],
        compiler_params=pltpu.CompilerParams(vmem_limit_bytes=8 * 2**20),
        cost_estimate=s.cost(1, 1, 1),
        name="scores_own" if own else "scores",
    )(queries, gain, keys)


def far_scores(lo, queries, out_grad, gain, keys, stats, nearest):
    s = Shapes(queries, keys)
    return pl.pallas_call(
        functools.partial(far_kernel, s.group),
        out_shape=[s.heads_array(), s.weight_array(), s.code_array(2)],
        grid_spec=pltpu.PrefetchScalarGridSpec(
            num_scalar_prefetch=1,
            grid=(s.kv_count,),
            in_specs=[s.wide, s.wide, s.line, s.thin] + [s.stat] * len(stats) + [s.heads],
            out_specs=[s.heads, s.weight, s.codes],
            scratch_shapes=[
                pltpu.VMEM((2 * s.rows, s.group * s.rows), jnp.bfloat16),
                pltpu.VMEM((s.group * s.rows, HD), jnp.bfloat16),
            ],
        ),
        compiler_params=pltpu.CompilerParams(vmem_limit_bytes=16 * 2**20),
        cost_estimate=s.cost(3, 1, 1),
        name="far_scores",
    )(lo, queries, out_grad, gain, keys, *stats, nearest)


def near_values(queries, keys, out_grad, weights, heads):
    s = Shapes(queries, keys)
    return pl.pallas_call(
        functools.partial(values_kernel, s.group),
        out_shape=[s.part_array()] * 2,
        grid=(s.kv_count,),
        in_specs=[s.wide, s.weight] + [s.heads] * 2,
        out_specs=[s.part] * 2,
        scratch_shapes=[
            pltpu.VMEM((2 * s.rows, s.group * s.rows), jnp.bfloat16),
            pltpu.VMEM((s.group * s.rows, HD), jnp.bfloat16),
        ],
        compiler_params=pltpu.CompilerParams(vmem_limit_bytes=15 * 2**20),
        cost_estimate=s.cost(1, 2, 0),
        name="near_values",
    )(out_grad, weights, *heads)


def attention_grads(first, count, before, queries, out_grad, gain, weights, heads, keys, values):
    s = Shapes(queries, keys[0], first)
    width = REACH * s.rows
    n_in = 4 + 3 * REACH
    return pl.pallas_call(
        functools.partial(grads_kernel, s.group, s.rows, len(before)),
        out_shape=[s.array(jnp.bfloat16, s.rows, s.channels)] * 2
        + [s.array(jnp.float32, 1, s.channels)]
        + [s.code_array(2), s.part_array(), s.part_array()],
        grid=(count,),
        in_specs=[s.wide, s.wide, s.line, s.weight]
        + [s.heads] * REACH
        + [s.thin] * (2 * REACH)
        + [pl.BlockSpec(memory_space=pl.ANY)] * len(before),
        out_specs=[s.wide, s.wide, s.line, s.codes, s.part, s.part],
        scratch_shapes=[
            pltpu.VMEM((HD, width), jnp.bfloat16),
            pltpu.VMEM((HD, width), jnp.bfloat16),
            pltpu.VMEM((width, HD), jnp.bfloat16),
            pltpu.VMEM((2, width, s.rows), jnp.bfloat16),
            pltpu.VMEM((width, s.group * s.rows), jnp.bfloat16),
            pltpu.VMEM((s.group * s.rows, HD), jnp.bfloat16),
        ],
        input_output_aliases={n_in + i: i for i in range(len(before))},
        compiler_params=pltpu.CompilerParams(vmem_limit_bytes=20 * 2**20),
        cost_estimate=s.cost(4, REACH, 0, count),
    )(queries, out_grad, gain, weights, *heads, *keys, *values, *before)


def step(queries, global_keys, global_values, out_grad, query_gain, doc_start):
    rows = queries.shape[1]
    device = lax.axis_index("ctx")
    q, do = queries[0], out_grad[0]
    gain = query_gain[None]
    together = lax.optimization_barrier
    lo = doc_start[0] * BLOCK - (device - (REACH - 1)) * rows
    lo, gain = together((lo, gain))
    own_keys, own_values = global_keys[0], global_values[0]
    near = [chunk_scores(q, gain, own_keys, True)]
    keys, values = [own_keys], [own_values]
    for i in range(1, REACH):
        keys.insert(0, shifted(keys[0], 1))
        if i < REACH - 1:
            near.insert(0, chunk_scores(q, gain, keys[0], False))
            values.insert(0, shifted(values[0], 1))
    values.insert(0, shifted(values[0], 1))
    most = own_keys.shape[1] // HD - 1

    stats = [stat for _, *pair in near for stat in pair]
    far, weights, dv_codes = far_scores(lo, q, do, gain, keys[0], stats, near[1][0])
    heads = [far] + [e for e, *_ in near]
    dv_codes = shifted(dv_codes, -1)
    dv_middle, dv_own = near_values(q, own_keys, do, weights, heads[1::2])
    early = attention_grads(0, most, [], q, do, gain, weights, heads, keys, values)
    dv_middle = shifted(hop([(dv_codes, 0)], dv_middle, False), -2)
    attn_out, query_grad, gain_term, dk_codes, dk_middle, dk_own = attention_grads(
        most, 1, early, q, do, gain, weights, heads, keys, values
    )
    dk_codes = shifted(dk_codes, -1)
    count = lax.axis_size("ctx")
    columns = [[i + z for i in range(0, count, Z_CHIPS)] for z in range(Z_CHIPS)]
    total = gathered_sum(gain_term, "dp", lax.axis_size("dp"))
    total = gathered_sum(total, "ctx", count // Z_CHIPS, columns)
    dk_middle = hop([(dk_codes, 0)], dk_middle, False)
    dk_middle = shifted(dk_middle, -2)
    gain_grad = ring_sum(total)
    value_grad = hop([(dv_middle, 0), (dv_codes, 1)], dv_own, True)
    key_grad = hop([(dk_middle, 0), (dk_codes, 1)], dk_own, True)
    return (
        attn_out[None],
        query_grad[None],
        key_grad[None],
        value_grad[None],
        gain_grad[0],
    )


def solution(mesh):
    rows = P("dp", "ctx", None)
    return jax.shard_map(
        step,
        mesh=mesh,
        in_specs=(rows, rows, rows, rows, P(), P("dp", "ctx")),
        out_specs=(rows, rows, rows, rows, P()),
        check_vma=False,
    )
```

```python
import functools
import math

import jax
import jax.numpy as jnp
from jax import lax
from jax.experimental import pallas as pl
from jax.experimental.pallas import tpu as pltpu
from jax.sharding import PartitionSpec as P


HD = 128
BLOCK = 128
REACH = 4
Z_CHIPS = 8
EXPONENT = 1.4426950408889634 / math.sqrt(HD)
SCALE_STEPS = 64.0
SCALE_ROWS = 16
CODE_MAX = 32767.0
CODE_ROWS = HD + SCALE_ROWS


def shifted(value, steps):
    count = lax.axis_size("ctx")
    first, last = (max(0, -steps), min(count, count - steps))
    pairs = [(source, source + steps) for source in range(first, last)]
    return lax.ppermute(value, "ctx", pairs)


def gathered_sum(value, axis, size, groups=None):
    copies = jnp.broadcast_to(value[None], (size, *value.shape))
    parts = lax.all_to_all(copies, axis, 0, 0, tiled=True, axis_index_groups=groups)
    return jnp.sum(parts, axis=0)


def ring_kernel(place, parts, out):
    count = parts.shape[0]
    total = parts[pl.ds(place[0], 1), :]
    for r in range(1, count):
        total = total + parts[pl.ds((place[0] + r) % count, 1), :]
    out[...] = total


def ring_sum(value):
    count = lax.axis_size("ctx")
    step = 1
    while step < Z_CHIPS:
        pairs = [
            (i, i - i % Z_CHIPS + (i + step) % Z_CHIPS) for i in range(count)
        ]
        moved = lax.ppermute(value, "ctx", pairs)
        value = jnp.concatenate([value, moved], axis=0)
        step *= 2
    place = (lax.axis_index("ctx") % Z_CHIPS).reshape(1)
    return pl.pallas_call(
        ring_kernel,
        out_shape=jax.ShapeDtypeStruct((1, value.shape[1]), jnp.float32),
        in_specs=[
            pl.BlockSpec(memory_space=pltpu.SMEM),
            pl.BlockSpec(memory_space=pltpu.VMEM),
        ],
        out_specs=pl.BlockSpec(memory_space=pltpu.VMEM),
        compiler_params=pltpu.CompilerParams(vmem_limit_bytes=4 * 2**20),
        name="ring_sum",
    )(place, value)


def encode(value):
    top = jnp.maximum(jnp.max(jnp.abs(value), axis=0, keepdims=True), 2.0**-100)
    level = jnp.ceil(jnp.log2(top) * SCALE_STEPS)
    coded = jnp.round(value * (jnp.exp2(level * (-1.0 / SCALE_STEPS)) * CODE_MAX))
    level = jnp.broadcast_to(level, (SCALE_ROWS, value.shape[1]))
    return tuple(v.astype(jnp.int32).astype(jnp.int16) for v in (coded, level))


def decode(coded, level):
    level = level.astype(jnp.int32).astype(jnp.float32)[:1]
    return coded.astype(jnp.int32).astype(jnp.float32) * (
        jnp.exp2(level * (1.0 / SCALE_STEPS)) * (1.0 / CODE_MAX)
    )


def dot(a, b, dims=((1,), (0,))):
    return lax.dot_general(a, b, (dims, ((), ())), preferred_element_type=jnp.float32)


def softened(raw):
    top = jnp.max(raw, axis=0, keepdims=True)
    e = jnp.exp2((raw - top) * EXPONENT)
    return e, top, jnp.sum(e, axis=0, keepdims=True)


def scaled_query(q_ref, gain_ref, cols):
    return (q_ref[:, cols].astype(jnp.float32) * gain_ref[:, cols]).astype(jnp.bfloat16)


def scores_kernel(group, own, q_ref, gain_ref, k_ref, e_ref, top_ref, sum_ref):
    rows = k_ref.shape[0]
    per = rows // BLOCK
    if own:
        key = lax.broadcasted_iota(jnp.int32, (BLOCK, rows), 0)
        query = lax.broadcasted_iota(jnp.int32, (BLOCK, rows), 1)
    for g in range(group):
        scaled = scaled_query(q_ref, gain_ref, slice(g * HD, (g + 1) * HD))
        for b in range(per):
            here = slice(b * BLOCK, (b + 1) * BLOCK)
            raw = dot(k_ref[here, :], scaled, ((1,), (1,)))
            if own:
                later = (key + b * BLOCK > query) & (query >= b * BLOCK)
                raw = jnp.where(later, -jnp.inf, raw)
            e, top, total = softened(raw)
            at = slice(g * per + b, g * per + b + 1)
            e_ref[g, here, :], top_ref[0, at, :], sum_ref[0, at, :] = e, top, total


def far_kernel(group, lo, q_ref, g_ref, gain_ref, k_ref, *refs):
    stats = refs[: 2 * (REACH - 1)]
    near_ref, e_ref, w_ref, dv_ref, p_low, g_all = refs[2 * (REACH - 1) :]
    rows = k_ref.shape[0]
    per = rows // BLOCK
    blocks = REACH * per
    half = lax.broadcasted_iota(jnp.int32, (1, rows), 1) // BLOCK
    begin = jnp.where(half == 0, lo[0], lo[1])
    allowed = [
        (begin <= b * BLOCK) & (half >= b - (REACH - 1) * per) for b in range(blocks)
    ]
    for g in range(group):
        cols = slice(g * HD, (g + 1) * HD)
        g_all[g * rows : (g + 1) * rows, :] = g_ref[:, cols]
        scaled = scaled_query(q_ref, gain_ref, cols)
        tops, sums = [], []
        for b in range(per):
            here = slice(b * BLOCK, (b + 1) * BLOCK)
            e, top, total = softened(dot(k_ref[here, :], scaled, ((1,), (1,))))
            e_ref[g, here, :] = e
            tops.append(top)
            sums.append(total)
        for j in range(REACH - 1):
            for b in range(per):
                at = slice(g * per + b, g * per + b + 1)
                tops.append(stats[2 * j][0, at, :])
                sums.append(stats[2 * j + 1][0, at, :])
        tops = [jnp.where(ok, top, -jnp.inf) for ok, top in zip(allowed, tops, strict=True)]
        highest = functools.reduce(jnp.maximum, tops)
        shares = [jnp.exp2((top - highest) * EXPONENT) for top in tops]
        total = sum(share * part for share, part in zip(shares, sums, strict=True))
        inverse = 1.0 / total
        for b in range(blocks):
            weight = shares[b] * inverse
            w_ref[0, g * blocks + b : g * blocks + b + 1, :] = weight
            chunk, b = b // per, b % per
            if chunk in (0, REACH - 2):
                here = slice(b * BLOCK, (b + 1) * BLOCK)
                e = (near_ref if chunk else e_ref)[g, here, :]
                at = (rows if chunk else 0) + b * BLOCK
                p_low[at : at + BLOCK, g * rows : (g + 1) * rows] = (e * weight).astype(
                    jnp.bfloat16
                )
    dv = dot(p_low[...], g_all[...])
    for i in range(2):
        part = dv[i * rows : (i + 1) * rows, :].T
        dv_ref[i, :HD, :], dv_ref[i, HD:, :] = encode(part)


def values_kernel(group, g_ref, w_ref, *refs):
    e_refs, dv_refs, (p_low, g_all) = refs[:2], refs[2:4], refs[4:]
    rows = g_ref.shape[0]
    per = rows // BLOCK
    blocks = REACH * per
    for g in range(group):
        g_all[g * rows : (g + 1) * rows, :] = g_ref[:, g * HD : (g + 1) * HD]
        for j, chunk in enumerate((1, REACH - 1)):
            for b in range(per):
                here = slice(b * BLOCK, (b + 1) * BLOCK)
                at = g * blocks + chunk * per + b
                probs = e_refs[j][g, here, :] * w_ref[0, at : at + 1, :]
                there = slice(j * rows + b * BLOCK, j * rows + (b + 1) * BLOCK)
                p_low[there, g * rows : (g + 1) * rows] = probs.astype(jnp.bfloat16)
    dv = dot(p_low[...], g_all[...])
    for j in range(2):
        dv_refs[j][...] = dv[j * rows : (j + 1) * rows, :].T


def grads_kernel(group, rows, skip, q_ref, g_ref, gain_ref, w_ref, *refs):
    e_refs, k_refs, v_refs = (refs[i * REACH : (i + 1) * REACH] for i in range(3))
    refs = refs[3 * REACH + skip :]
    o_ref, dq_ref, gain_out, *dk_refs = refs[:6]
    k_t, v_t, v_all, p_all, ds_all, q_all = refs[6:]
    per = rows // BLOCK
    blocks = REACH * per
    factor = 1.0 / math.sqrt(HD)
    for j in range(REACH):
        part = slice(j * rows, (j + 1) * rows)
        v_all[part, :] = v_refs[j][...]
        k_t[:, part] = k_refs[j][...].T
        v_t[:, part] = v_refs[j][...].T

    def probs_of(g, b):
        here = slice(b % per * BLOCK, (b % per + 1) * BLOCK)
        at = g * blocks + b
        return e_refs[b // per][g, here, :] * w_ref[0, at : at + 1, :]

    for g in range(group):
        cols = slice(g * HD, (g + 1) * HD)
        mine = slice(g * rows, (g + 1) * rows)
        q32 = q_ref[:, cols].astype(jnp.float32)
        gain = gain_ref[:, cols]
        q_all[mine, :] = (q32 * gain).astype(jnp.bfloat16)
        for b in range(blocks):
            p_all[g % 2, b * BLOCK : (b + 1) * BLOCK, :] = probs_of(g, b).astype(jnp.bfloat16)
        out_t = dot(v_t[...], p_all[g % 2]).astype(jnp.bfloat16)
        o_ref[:, cols] = out_t.T
        g_t = g_ref[:, cols].T
        delta = jnp.sum(g_t.astype(jnp.float32) * out_t.astype(jnp.float32), axis=0, keepdims=True)
        for b in range(blocks):
            here = slice(b * BLOCK, (b + 1) * BLOCK)
            ds = probs_of(g, b) * (dot(v_all[here, :], g_t) - delta)
            ds_all[here, mine] = ds.astype(jnp.bfloat16)
        dscaled = (dot(k_t[...], ds_all[:, mine]) * factor).T
        dq_ref[:, cols] = (dscaled * gain).astype(jnp.bfloat16)
        gain_out[:, cols] = jnp.sum(dscaled * q32, axis=0, keepdims=True)
    dk = dot(ds_all[...], q_all[...]) * factor
    dk_codes, dk_middle, dk_own = dk_refs
    far, middle, nearest, own = (dk[j * rows : (j + 1) * rows, :].T for j in range(REACH))
    dk_middle[...], dk_own[...] = middle, own
    for i, part in enumerate((far, nearest)):
        dk_codes[i, :HD, :], dk_codes[i, HD:, :] = encode(part)


def hop_kernel(kv_count, picks, last, *refs):
    *messages, part, out = refs
    for c in range(kv_count):
        at, here = c * CODE_ROWS, slice(c * HD, (c + 1) * HD)
        total = part[here, :]
        for message, pick in zip(messages, picks, strict=True):
            total = total + decode(
                message[pick, at : at + HD, :], message[pick, at + HD : at + CODE_ROWS, :]
            )
        if last:
            out[:, here] = total.T.astype(jnp.bfloat16)
        else:
            out[0, at : at + HD, :], out[0, at + HD : at + CODE_ROWS, :] = encode(total)


def hop(messages, part, last):
    kv_channels, rows = part.shape
    messages, picks = zip(*messages, strict=True)
    shape = (
        jax.ShapeDtypeStruct((rows, kv_channels), jnp.bfloat16)
        if last
        else jax.ShapeDtypeStruct((1, *messages[0].shape[1:]), jnp.int16)
    )
    return pl.pallas_call(
        functools.partial(hop_kernel, kv_channels // HD, picks, last),
        out_shape=jax.ShapeDtypeStruct(shape.shape, shape.dtype),
        compiler_params=pltpu.CompilerParams(vmem_limit_bytes=8 * 2**20),
        cost_estimate=pl.CostEstimate(
            flops=10 * part.size, bytes_accessed=8 * part.size, transcendentals=0
        ),
        name="last_hop" if last else "hop",
    )(*messages, part)


class Shapes:
    def __init__(self, queries, keys, first=0):
        self.rows, self.channels = queries.shape
        self.kv_channels = keys.shape[1]
        self.kv_count = self.kv_channels // HD
        self.group = self.channels // self.kv_channels
        self.blocks = REACH * self.rows // BLOCK
        self.stat_rows = self.group * self.rows // BLOCK
        rows, group = self.rows, self.group
        self.wide = pl.BlockSpec((rows, group * HD), lambda c, *_: (0, c + first))
        self.line = pl.BlockSpec((1, group * HD), lambda c, *_: (0, c + first))
        self.thin = pl.BlockSpec((rows, HD), lambda c, *_: (0, c + first))
        self.code, self.codes = (
            pl.BlockSpec((n, CODE_ROWS, rows), lambda c, *_: (0, c + first, 0)) for n in (1, 2)
        )
        self.part = pl.BlockSpec((HD, rows), lambda c, *_: (c + first, 0))
        self.heads = pl.BlockSpec((group, rows, rows), lambda c, *_: (c + first, 0, 0))
        self.stat = pl.BlockSpec((1, self.stat_rows, rows), lambda c, *_: (c + first, 0, 0))
        self.weight = pl.BlockSpec(
            (1, group * self.blocks, rows), lambda c, *_: (c + first, 0, 0)
        )

    def array(self, dtype, *shape):
        return jax.ShapeDtypeStruct(shape, dtype)

    def heads_array(self):
        return self.array(jnp.float32, self.kv_count * self.group, self.rows, self.rows)

    def stat_array(self):
        return self.array(jnp.float32, self.kv_count, self.stat_rows, self.rows)

    def weight_array(self):
        return self.array(jnp.float32, self.kv_count, self.group * self.blocks, self.rows)

    def code_array(self, count=1):
        return self.array(jnp.int16, count, self.kv_count * CODE_ROWS, self.rows)

    def part_array(self):
        return self.array(jnp.float32, self.kv_channels, self.rows)

    def cost(self, products, chunks, exps, count=None):
        heads = (self.kv_count if count is None else count) * self.group
        size = heads * chunks * self.rows * self.rows
        return pl.CostEstimate(
            flops=2 * products * size * HD, bytes_accessed=4 * size, transcendentals=exps * size
        )


def chunk_scores(queries, gain, keys, own):
    s = Shapes(queries, keys)
    return pl.pallas_call(
        functools.partial(scores_kernel, s.group, own),
        out_shape=[s.heads_array(), s.stat_array(), s.stat_array()],
        grid=(s.kv_count,),
        in_specs=[s.wide, s.line, s.thin],
        out_specs=[s.heads, s.stat, s.stat],
        compiler_params=pltpu.CompilerParams(vmem_limit_bytes=8 * 2**20),
        cost_estimate=s.cost(1, 1, 1),
        name="scores_own" if own else "scores",
    )(queries, gain, keys)


def far_scores(lo, queries, out_grad, gain, keys, stats, nearest):
    s = Shapes(queries, keys)
    return pl.pallas_call(
        functools.partial(far_kernel, s.group),
        out_shape=[s.heads_array(), s.weight_array(), s.code_array(2)],
        grid_spec=pltpu.PrefetchScalarGridSpec(
            num_scalar_prefetch=1,
            grid=(s.kv_count,),
            in_specs=[s.wide, s.wide, s.line, s.thin] + [s.stat] * len(stats) + [s.heads],
            out_specs=[s.heads, s.weight, s.codes],
            scratch_shapes=[
                pltpu.VMEM((2 * s.rows, s.group * s.rows), jnp.bfloat16),
                pltpu.VMEM((s.group * s.rows, HD), jnp.bfloat16),
            ],
        ),
        compiler_params=pltpu.CompilerParams(vmem_limit_bytes=16 * 2**20),
        cost_estimate=s.cost(3, 1, 1),
        name="far_scores",
    )(lo, queries, out_grad, gain, keys, *stats, nearest)


def near_values(queries, keys, out_grad, weights, heads):
    s = Shapes(queries, keys)
    return pl.pallas_call(
        functools.partial(values_kernel, s.group),
        out_shape=[s.part_array(), pltpu.HBM((s.kv_channels, s.rows), jnp.float32)],
        grid=(s.kv_count,),
        in_specs=[s.wide, s.weight] + [s.heads] * 2,
        out_specs=[s.part] * 2,
        scratch_shapes=[
            pltpu.VMEM((2 * s.rows, s.group * s.rows), jnp.bfloat16),
            pltpu.VMEM((s.group * s.rows, HD), jnp.bfloat16),
        ],
        compiler_params=pltpu.CompilerParams(vmem_limit_bytes=15 * 2**20),
        cost_estimate=s.cost(1, 2, 0),
        name="near_values",
    )(out_grad, weights, *heads)


def attention_grads(first, count, before, queries, out_grad, gain, weights, heads, keys, values):
    s = Shapes(queries, keys[0], first)
    width = REACH * s.rows
    n_in = 4 + 3 * REACH
    return pl.pallas_call(
        functools.partial(grads_kernel, s.group, s.rows, len(before)),
        out_shape=[s.array(jnp.bfloat16, s.rows, s.channels)] * 2
        + [s.array(jnp.float32, 1, s.channels)]
        + [s.code_array(2), s.part_array(), s.part_array()],
        grid=(count,),
        in_specs=[s.wide, s.wide, s.line, s.weight]
        + [s.heads] * REACH
        + [s.thin] * (2 * REACH)
        + [pl.BlockSpec(memory_space=pl.ANY)] * len(before),
        out_specs=[s.wide, s.wide, s.line, s.codes, s.part, s.part],
        scratch_shapes=[
            pltpu.VMEM((HD, width), jnp.bfloat16),
            pltpu.VMEM((HD, width), jnp.bfloat16),
            pltpu.VMEM((width, HD), jnp.bfloat16),
            pltpu.VMEM((2, width, s.rows), jnp.bfloat16),
            pltpu.VMEM((width, s.group * s.rows), jnp.bfloat16),
            pltpu.VMEM((s.group * s.rows, HD), jnp.bfloat16),
        ],
        input_output_aliases={n_in + i: i for i in range(len(before))},
        compiler_params=pltpu.CompilerParams(vmem_limit_bytes=20 * 2**20),
        cost_estimate=s.cost(4, REACH, 0, count),
    )(queries, out_grad, gain, weights, *heads, *keys, *values, *before)


def step(queries, global_keys, global_values, out_grad, query_gain, doc_start):
    rows = queries.shape[1]
    device = lax.axis_index("ctx")
    q, do = queries[0], out_grad[0]
    gain = query_gain[None]
    together = lax.optimization_barrier
    lo = doc_start[0] * BLOCK - (device - (REACH - 1)) * rows
    lo, gain = together((lo, gain))
    own_keys, own_values = global_keys[0], global_values[0]
    near = [chunk_scores(q, gain, own_keys, True)]
    keys, values = [own_keys], [own_values]
    for i in range(1, REACH):
        keys.insert(0, shifted(keys[0], 1))
        if i < REACH - 1:
            near.insert(0, chunk_scores(q, gain, keys[0], False))
            values.insert(0, shifted(values[0], 1))
    values.insert(0, shifted(values[0], 1))
    most = own_keys.shape[1] // HD - 1

    stats = [stat for _, *pair in near for stat in pair]
    far, weights, dv_codes = far_scores(lo, q, do, gain, keys[0], stats, near[1][0])
    heads = [far] + [e for e, *_ in near]
    dv_codes = shifted(dv_codes, -1)
    dv_middle, dv_own = near_values(q, own_keys, do, weights, heads[1::2])
    early = attention_grads(0, most, [], q, do, gain, weights, heads, keys, values)
    dv_middle = shifted(hop([(dv_codes, 0)], dv_middle, False), -2)
    attn_out, query_grad, gain_term, dk_codes, dk_middle, dk_own = attention_grads(
        most, 1, early, q, do, gain, weights, heads, keys, values
    )
    dk_codes = shifted(dk_codes, -1)
    count = lax.axis_size("ctx")
    columns = [[i + z for i in range(0, count, Z_CHIPS)] for z in range(Z_CHIPS)]
    total = gathered_sum(gain_term, "dp", lax.axis_size("dp"))
    total = gathered_sum(total, "ctx", count // Z_CHIPS, columns)
    dk_middle = hop([(dk_codes, 0)], dk_middle, False)
    dk_middle = shifted(dk_middle, -2)
    gain_grad = ring_sum(total)
    value_grad = hop([(dv_middle, 0), (dv_codes, 1)], dv_own, True)
    key_grad = hop([(dk_middle, 0), (dk_codes, 1)], dk_own, True)
    return (
        attn_out[None],
        query_grad[None],
        key_grad[None],
        value_grad[None],
        gain_grad[0],
    )


def solution(mesh):
    rows = P("dp", "ctx", None)
    return jax.shard_map(
        step,
        mesh=mesh,
        in_specs=(rows, rows, rows, rows, P(), P("dp", "ctx")),
        out_specs=(rows, rows, rows, rows, P()),
        check_vma=False,
    )
```
